128 devices in a mesh: gx: 8 (over z, core), gy: 16 (over y, x).
Axes of the slice: x: 4, y: 4, z: 4, core: 2. Of those that a mesh axis runs over, the one named last changes fastest.
Arguments:
- velocity: float32 [3, 64, 512, 1024], P(None, None, 'gy', 'gx'), may hold values from -6 to 6
- pressure: float32 [64, 512, 1024], P(None, 'gy', 'gx'), may hold values from -6 to 6
- memory: float32 [64, 512, 1024], P(None, 'gy', 'gx'), may hold values from -4 to 4
- buoyancy: float32 [64, 512, 1024], P(None, 'gy', 'gx'), may hold values from 0.1 to 0.4
- modulus: float32 [64, 512, 1024], P(None, 'gy', 'gx'), may hold values from 0.1 to 0.4
- relax: float32 [64, 512, 1024], P(None, 'gy', 'gx'), may hold values from 0.05 to 0.5
- strength: float32 [64, 512, 1024], P(None, 'gy', 'gx'), may hold values from 0.2 to 1
- spectra: float32 [32768, 256], P(('gx', 'gy')), may hold values from -6 to 6
- patch_cell: int32 [32768], P(('gx', 'gy')), may hold values from 0 to 262143
- rupture_patches: int32 [64, 512], replicated, may hold values from -1 to 32767, as said below
- slip_weights: bfloat16 [64, 512, 512], P('gx', 'gy'), may hold values from -0.375 to 0.375
Outputs:
- velocity_out: float32 [3, 64, 512, 1024], P(None, None, 'gy', 'gx')
- pressure_out: float32 [64, 512, 1024], P(None, 'gy', 'gx')
- memory_out: float32 [64, 512, 1024], P(None, 'gy', 'gx')
- spectra_out: float32 [32768, 256], P(('gx', 'gy'))
- slip_response: float32 [64, 512, 256], P('gx', 'gy')
The draws below stay inside these ranges and needn't reach their ends.
Inputs may be any that keep to these rules, and one draw needn't show every extreme that they name: `patch_cell`: the cell of a patch is a flat index (z * 32 + y) * 128 + x within its brick. `rupture_patches`: each patch is listed in at most one slot. Slot (r, s) belongs to the owner at index r // 8 of gx and s // 32 of gy; of the 256 patches of one block, at most 2 are listed in the slots of any one owner, and some pairs of block and owner reach 2.
All inputs are finite; a program needn't handle non-finite values.
Results may differ from the reference program's by a relative error of at most 0.0029.
Values may be sent and summed in bfloat16 or wider, within the bound.
No kernel may reach another device: no remote copies, remote signals or barrier semaphores. Data moves between devices by JAX's collectives and lax.ppermute only.
A program may use at most 128 MiB of HBM per device.

```python
import math
import jax
import jax.numpy as jnp
from jax import lax

CX = 128
CY = 32
CZ = 64
STEPS = 4
FREQS = 128
VARS = 512
CAP = 2
RUP_GROUP = 8
PATCH_DEV = 256
NX = 1024
NY = 512
PATCHES = 32768
SLOT_DEV = 32
SLOTS = 512
RUPTURES = 64
N_GY = 16


def draw_rupture_patches(key, part):
    devs = PATCHES // PATCH_DEV
    groups_y = SLOTS // SLOT_DEV
    keys = jax.random.split(jax.random.fold_in(key, 7), 7)
    sigma = jax.random.permutation(keys[0], devs)
    tau = jax.random.permutation(keys[1], devs)
    offsets = jax.random.permutation(keys[2], devs)[:PATCH_DEV // CAP]
    position = jnp.arange(PATCH_DEV, dtype=jnp.int32)
    group_of = position // CAP
    target = sigma[(tau[:, None] + offsets[None, :]) % devs]
    target_pos = target[:, group_of]
    order = jax.vmap(lambda k: jax.random.permutation(k, PATCH_DEV))(jax.random.split(keys[3], devs))
    patch_global = jnp.arange(devs, dtype=jnp.int32)[:, None] * PATCH_DEV + order.astype(jnp.int32)
    slot_perm = jax.vmap(lambda k: jax.random.permutation(k, PATCH_DEV))(jax.random.split(keys[4], devs))
    local = slot_perm[target_pos, position[None, :]]
    levels = jnp.array([100, 100, 100, 50], dtype=jnp.int32)
    heat = levels[jax.random.randint(keys[5], (devs,), 0, 4)]
    heat = heat.at[sigma[0]].set(100)
    keep = jax.random.randint(keys[6], (devs, PATCH_DEV), 0, 100) < heat[target_pos]
    row = target_pos // groups_y * RUP_GROUP + local // SLOT_DEV
    col = target_pos % groups_y * SLOT_DEV + local % SLOT_DEV
    flat = row * SLOTS + col
    total = RUPTURES * SLOTS
    table = jnp.full((total + 1,), -1, dtype=jnp.int32)
    table = table.at[jnp.where(keep, flat, total).reshape(-1)].set(patch_global.reshape(-1))
    return table[:total].reshape(RUPTURES, SLOTS)


def place_ends(values, own_key, least, top_value):
    place = [jax.random.randint(jax.random.fold_in(own_key, axis), (), 0, length) for axis, length in enumerate(values.shape)]
    longest = values.shape.index(max(values.shape))
    neighbour = place[:longest] + [(place[longest] + 1) % values.shape[longest]] + place[longest + 1:]
    return values.at[tuple(place)].set(least).at[tuple(neighbour)].set(top_value)


def with_spikes(values, own_key, source, target, parts, factor):
    owner, partner = [(jnp.arange(values.shape[dim]) // (values.shape[dim] // parts)).reshape([-1 if axis == dim else 1 for axis in range(values.ndim)]) for dim in (source, target)]
    chosen = jax.random.permutation(own_key, parts)[partner]
    strong = (owner == chosen) | (owner == (partner + parts // 2) % parts)
    return jnp.where(strong, factor * values, values)


def block_levels(key, shape, cuts, least, largest):
    level = 1.0
    for dim, shards_of in cuts:
        heights = jax.random.uniform(jax.random.fold_in(jax.random.fold_in(key, 6), dim), (shards_of,), jnp.float32, least / len(cuts), largest / len(cuts))
        level = level * jnp.repeat(jnp.exp(heights), shape[dim] // shards_of).reshape((-1,) + (1,) * (len(shape) - 1 - dim))
    return level


def scatter_about(own_key, shape, scale, reach, pieces=(), kind=jnp.bfloat16):
    values = jax.random.normal(own_key, shape, jnp.float32) * scale
    if len(pieces) > 0:
        values = block_levels(own_key, shape, pieces, -0.22, 0.18) * values
    return jnp.clip(values, min=-reach, max=reach).astype(kind)


def noise_with(rng, dims, scale, bound, cuts, heavy, kind=jnp.bfloat16):
    values = scale * jax.random.normal(rng, dims, jnp.float32)
    if cuts:
        values = values * block_levels(rng, dims, cuts, -0.22, 0.18)
    return jnp.clip(with_spikes(values, jax.random.fold_in(rng, 3), *heavy), -bound, bound).astype(kind)


def setup_inputs(seed: int = 0) -> dict:
    splits = jax.random.split(jax.random.key(seed), 12)
    velocity = scatter_about(splits[0], (3, CZ, NY, NX), 1.0, 6.0, ((2, 16), (3, 8)), jnp.float32)
    pressure = scatter_about(splits[1], (CZ, NY, NX), 1.0, 6.0, ((1, 16), (2, 8)), jnp.float32)
    memory = scatter_about(splits[2], (CZ, NY, NX), 0.3, 4.0, ((1, 16), (2, 8)), jnp.float32)
    buoyancy = jnp.clip(jnp.exp(math.log(0.4) - 1.3862944 * jax.random.uniform(splits[3], (CZ, NY, NX), jnp.float32) ** block_levels(splits[3], (CZ, NY, NX), ((1, 16), (2, 8)), -0.2, 0.2)), 0.1, 0.4)
    modulus = jnp.clip(jnp.exp(math.log(0.4) - 1.3862944 * jax.random.uniform(splits[4], (CZ, NY, NX), jnp.float32) ** block_levels(splits[4], (CZ, NY, NX), ((1, 16), (2, 8)), -0.2, 0.2)), 0.1, 0.4)
    relax = jnp.clip(jnp.exp(math.log(0.5) - 2.3025851 * jax.random.uniform(splits[5], (CZ, NY, NX), jnp.float32) ** block_levels(splits[5], (CZ, NY, NX), ((1, 16), (2, 8)), -0.2, 0.2)), 0.05, 0.5)
    strength = jnp.clip(0.2 + 0.8 * jax.random.uniform(splits[6], (CZ, NY, NX), jnp.float32) ** block_levels(splits[6], (CZ, NY, NX), ((1, 16), (2, 8)), -0.2, 0.2), 0.2, 1.0)
    spectra = scatter_about(splits[7], (PATCHES, 2 * FREQS), 1.0, 6.0, ((0, 128),), jnp.float32)
    patch_cell = place_ends(jax.random.randint(splits[8], (PATCHES,), 0, CX * CY * CZ), jax.random.fold_in(splits[8], 1), 0, (CX * CY * CZ) - 1).astype(jnp.int32)
    rupture_patches = draw_rupture_patches(jax.random.fold_in(splits[11], 71), 0)
    slip_weights = noise_with(splits[10], (RUPTURES, SLOTS, VARS), SLOTS ** -0.5, 0.375, ((0, 8), (1, 16)), (1, 2, 16, 2.0))
    return {"velocity": velocity, "pressure": pressure, "memory": memory, "buoyancy": buoyancy, "modulus": modulus, "relax": relax, "strength": strength, "spectra": spectra, "patch_cell": patch_cell, "rupture_patches": rupture_patches, "slip_weights": slip_weights}


def centred(field, axis):
    widths = [(0, 0), (0, 0), (0, 0)]
    widths[axis] = (1, 1)
    padded = jnp.pad(field, widths)
    length = field.shape[axis]
    return lax.slice_in_dim(padded, 2, length + 2, axis=axis) - lax.slice_in_dim(padded, 0, length, axis=axis)


def phase_row(freqs, step):
    angle = jnp.pi * (jnp.arange(freqs, dtype=jnp.float32) + 0.5) / freqs * step
    return jnp.concatenate([jnp.cos(angle), -jnp.sin(angle)])


def reference(velocity, pressure, memory, buoyancy, modulus, relax, strength, spectra, patch_cell, rupture_patches, slip_weights):
    speed_x, speed_y, speed_z = velocity[0], velocity[1], velocity[2]
    freqs = spectra.shape[1] // 2
    block = jnp.arange(spectra.shape[0], dtype=jnp.int32) // PATCH_DEV
    col_block = block // N_GY
    row_block = block % N_GY
    depth = patch_cell // (CY * CX)
    rows = row_block * CY + (patch_cell // CX) % CY
    cols = col_block * CX + patch_cell % CX
    for step in range(STEPS):
        speed_x = speed_x - buoyancy * centred(pressure, 2)
        speed_y = speed_y - buoyancy * centred(pressure, 1)
        speed_z = speed_z - buoyancy * centred(pressure, 0)
        spread = centred(speed_x, 2) + centred(speed_y, 1) + centred(speed_z, 0)
        shear = centred(speed_x, 1) + centred(speed_y, 2)
        memory = memory - relax * (memory + strength * spread)
        pressure = pressure - modulus * (spread + memory)
        sample = shear[depth, rows, cols]
        spectra = spectra + sample[:, None] * phase_row(freqs, step + 1)[None, :]
    live = rupture_patches >= 0
    picked = spectra[jnp.where(live, rupture_patches, 0)]
    slot_spectra = jnp.where(live[:, :, None], picked, jnp.zeros_like(picked)).astype(jnp.bfloat16)
    slip = jnp.einsum("rsv,rsf->rvf", slip_weights.astype(jnp.float32), slot_spectra.astype(jnp.float32))
    velocity_out = jnp.stack([speed_x, speed_y, speed_z])
    return velocity_out, pressure, memory, spectra, slip
```

```python
import functools

import jax
import jax.numpy as jnp
from jax import lax
from jax.experimental import pallas as pl
from jax.experimental.pallas import tpu as pltpu
from jax.sharding import PartitionSpec as P

STEPS = 4
CAP = 2
NZ, NY, NX = 64, 32, 128
HALO = 8
EY = NY + 2 * HALO
FIELDS = 9
VX, VY, VZ, PR, ME, BU, MO, RE, ST = range(FIELDS)


def lanes(shape):
    return lax.broadcasted_iota(jnp.int32, shape, len(shape) - 1)


def roll(x, shift, axis=1):
    shift = shift % x.shape[axis]
    return pltpu.roll(x, shift, axis) if shift else x


def pack_kernel(vel, pr, me, bu, mo, re, st, lo_ref, hi_ref, q_ref):
    lane = lanes((NY, 128))
    fields = [vel.at[0], vel.at[1], vel.at[2], pr, me, bu, mo, re, st]
    for f, ref in enumerate(fields):
        lows, highs = [], []
        strip = jnp.zeros((NY, 128), jnp.float32)
        for g in range(8):
            plane = ref[g, 0]
            lows.append(plane[:HALO])
            highs.append(plane[NY - HALO :])
            strip = jnp.where((lane >> 4) == g, roll(plane, 8 + 16 * g), strip)
        lo_ref[0, f] = jnp.concatenate(lows, axis=0).astype(jnp.bfloat16)
        hi_ref[0, f] = jnp.concatenate(highs, axis=0).astype(jnp.bfloat16)
        q_ref[0, f] = strip.astype(jnp.bfloat16)


def pack(velocity, *fields):
    spec = pl.BlockSpec((8, 1, NY, NX), lambda i: (0, i, 0, 0))
    vspec = pl.BlockSpec((3, 8, 1, NY, NX), lambda i: (0, 0, i, 0, 0))
    yspec = pl.BlockSpec((1, FIELDS, 64, 128), lambda i: (i, 0, 0, 0))
    qspec = pl.BlockSpec((1, FIELDS, NY, 128), lambda i: (i, 0, 0, 0))
    yshape = jax.ShapeDtypeStruct((8, FIELDS, 64, 128), jnp.bfloat16)
    qshape = jax.ShapeDtypeStruct((8, FIELDS, NY, 128), jnp.bfloat16)
    return pl.pallas_call(
        pack_kernel,
        out_shape=(yshape, yshape, qshape),
        grid=(8,),
        in_specs=[vspec] + [spec] * 6,
        out_specs=(yspec, yspec, qspec),
        name="pack",
    )(velocity.reshape(3, 8, 8, NY, NX), *[f.reshape(8, 8, NY, NX) for f in fields])


def shifted(array, axis, up):
    n = lax.axis_size(axis)
    pairs = [(i, i + 1) if up else (i + 1, i) for i in range(n - 1)]
    return lax.ppermute(array, axis, pairs)


def swap_edges(x, low):
    return jnp.where(low, roll(x, -1), roll(x, 1))


def ydiff(x):
    return roll(x, -1, 0) - roll(x, 1, 0)


def steps_kernel(
    cell,
    vel,
    pr,
    me,
    bu,
    mo,
    re,
    st,
    spectra,
    phase,
    lane_of,
    yprev,
    ynext,
    side,
    cprev,
    cnext,
    vel_o,
    pr_o,
    me_o,
    spec_o,
    E,
    S,
    shear,
    G,
    sems,
):
    inside = pl.ds(HALO, NY)
    zin = pl.ds(1, NZ)
    sources = [vel.at[0], vel.at[1], vel.at[2], pr, me, bu, mo, re, st]
    copies = [
        pltpu.make_async_copy(src, E.at[f, zin, inside, :], sems.at[f])
        for f, src in enumerate(sources)
    ]
    for c in copies:
        c.start()
    lane = lanes((EY, 128))
    lane16 = lane & 15
    group = lane >> 4
    low = lane16 <= 7
    zero = jnp.zeros((EY, 128), jnp.float32)
    for f in (VZ, PR):
        E[f, 0] = zero
        E[f, NZ + 1] = zero

    def fill(zi, _):
        cp = cprev[zi].astype(jnp.float32)
        cn = cnext[zi].astype(jnp.float32)
        for f in range(FIELDS):
            yp = yprev[zi, f].astype(jnp.float32)
            yn = ynext[zi, f].astype(jnp.float32)
            for g in range(8):
                z = g * 8 + zi + 1
                E[f, z, :HALO] = yp[8 * g : 8 * g + 8]
                E[f, z, HALO + NY :] = yn[8 * g : 8 * g + 8]
            S[f, zi + 1, HALO : HALO + NY] = side[zi, f].astype(jnp.float32)
            S[f, zi + 1, :HALO] = cp[8 * f : 8 * f + 8]
            S[f, zi + 1, HALO + NY :] = cn[8 * f : 8 * f + 8]
        return 0

    lax.fori_loop(0, 8, fill, 0)

    def wrap_planes(f):
        S[f, 0] = jnp.where(lane < 16, 0.0, roll(S[f, 8], 16))
        S[f, 9] = jnp.where(lane >= 112, 0.0, roll(S[f, 1], -16))

    wrap_planes(PR)
    spec_o[...] = spectra[...]
    for c in copies:
        c.wait()

    def velocities(zi, _):
        zs = zi + 1
        edge = swap_edges(S[PR, zs], low)
        join = zero
        for g in range(8):
            z = g * 8 + zi + 1
            p0 = E[PR, z]
            halo = roll(edge, 120 - 16 * g)
            dx = jnp.where(lane == 127, halo, roll(p0, -1)) - jnp.where(lane == 0, halo, roll(p0, 1))
            b = E[BU, z]
            E[VX, z] = E[VX, z] - b * dx
            E[VY, z] = E[VY, z] - b * ydiff(p0)
            E[VZ, z] = E[VZ, z] - b * (E[PR, z + 1] - E[PR, z - 1])
            join = jnp.where(group == g, roll(p0, 16 * g + 8), join)
        join = swap_edges(join, low)
        ps = S[PR, zs]
        b = S[BU, zs]
        dx = jnp.where(lane16 == 7, join, roll(ps, -1)) - jnp.where(lane16 == 8, join, roll(ps, 1))
        S[VX, zs] = S[VX, zs] - b * dx
        S[VY, zs] = S[VY, zs] - b * ydiff(ps)
        S[VZ, zs] = S[VZ, zs] - b * (S[PR, zs + 1] - S[PR, zs - 1])
        return 0

    def updated(ref, z, spread):
        m = ref[ME, z]
        m = m - ref[RE, z] * (m + ref[ST, z] * spread)
        ref[ME, z] = m
        ref[PR, z] = ref[PR, z] - ref[MO, z] * (spread + m)

    def pressures(zi, _):
        zs = zi + 1
        edge_x = swap_edges(S[VX, zs], low)
        edge_y = swap_edges(S[VY, zs], low)[HALO : HALO + NY]
        join = zero
        lane_in = lane[:NY]
        for g in range(8):
            z = g * 8 + zi + 1
            vx, vy = E[VX, z], E[VY, z]
            halo = roll(edge_x, 120 - 16 * g)
            dx = jnp.where(lane == 127, halo, roll(vx, -1)) - jnp.where(lane == 0, halo, roll(vx, 1))
            spread = dx + ydiff(vy) + (E[VZ, z + 1] - E[VZ, z - 1])
            updated(E, z, spread)
            vy = vy[HALO : HALO + NY]
            halo = roll(edge_y, 120 - 16 * g)
            dx = jnp.where(lane_in == 127, halo, roll(vy, -1)) - jnp.where(
                lane_in == 0, halo, roll(vy, 1)
            )
            row = pl.multiple_of((g * 8 + zi) * NY, NY)
            shear[pl.ds(row, NY), :] = ydiff(vx)[HALO : HALO + NY] + dx
            join = jnp.where(group == g, roll(vx, 16 * g + 8), join)
        join = swap_edges(join, low)
        vx, vy = S[VX, zs], S[VY, zs]
        dx = jnp.where(lane16 == 7, join, roll(vx, -1)) - jnp.where(lane16 == 8, join, roll(vx, 1))
        updated(S, zs, dx + ydiff(vy) + (S[VZ, zs + 1] - S[VZ, zs - 1]))
        return 0

    wanted = lanes((256, 128)) == lane_of[...]

    def step(n, _):
        lax.fori_loop(0, 8, velocities, 0)
        wrap_planes(VZ)
        lax.fori_loop(0, 8, pressures, 0)
        wrap_planes(PR)

        def pick(i, _):
            for k in range(8):
                c = cell[i * 8 + k]
                G[pl.ds(i * 8 + k, 1), :] = shear[pl.ds(c >> 7, 1), :]
            return 0

        lax.fori_loop(0, 32, pick, 0)
        sample = jnp.sum(jnp.where(wanted, G[...], 0.0), axis=1, keepdims=True)
        spec_o[...] = spec_o[...] + sample * phase[pl.ds(n, 1), :]
        return 0

    lax.fori_loop(0, STEPS, step, 0)
    outs = [
        pltpu.make_async_copy(E.at[f, zin, inside, :], dst, sems.at[f])
        for f, dst in enumerate([vel_o.at[0], vel_o.at[1], vel_o.at[2], pr_o, me_o])
    ]
    for c in outs:
        c.start()
    for c in outs:
        c.wait()


def phase_rows(freqs):
    rows = []
    for step in range(1, STEPS + 1):
        angle = jnp.pi * (jnp.arange(freqs, dtype=jnp.float32) + 0.5) / freqs * step
        rows.append(jnp.concatenate([jnp.cos(angle), -jnp.sin(angle)]))
    return jnp.stack(rows)


def four_steps(velocity, fields, spectra, patch_cell, halos):
    any_spec = pl.BlockSpec(memory_space=pl.ANY)
    vmem = pl.BlockSpec(memory_space=pltpu.VMEM)
    smem = pl.BlockSpec(memory_space=pltpu.SMEM)
    field = jax.ShapeDtypeStruct((NZ, NY, NX), jnp.float32)
    return pl.pallas_call(
        steps_kernel,
        out_shape=(
            jax.ShapeDtypeStruct(velocity.shape, jnp.float32),
            field,
            field,
            jax.ShapeDtypeStruct(spectra.shape, jnp.float32),
        ),
        in_specs=[smem] + [any_spec] * 7 + [vmem] * 8,
        out_specs=(any_spec, any_spec, any_spec, vmem),
        scratch_shapes=[
            pltpu.VMEM((FIELDS, NZ + 2, EY, 128), jnp.float32),
            pltpu.VMEM((FIELDS, 10, EY, 128), jnp.float32),
            pltpu.VMEM((NZ * NY, 128), jnp.float32),
            pltpu.VMEM((256, 128), jnp.float32),
            pltpu.SemaphoreType.DMA((FIELDS,)),
        ],
        compiler_params=pltpu.CompilerParams(vmem_limit_bytes=40 * 1024 * 1024),
        name="four_steps",
    )(
        patch_cell,
        velocity,
        *fields,
        spectra,
        phase_rows(spectra.shape[1] // 2),
        (patch_cell & 127)[:, None],
        *halos,
    )


def halo_exchange(velocity, fields):
    lo, hi, q = pack(velocity, *fields)
    yprev = shifted(hi, "gy", True)
    ynext = shifted(lo, "gy", False)
    left = shifted(q, "gx", True)
    right = shifted(q, "gx", False)
    side = jnp.where((jnp.arange(128) & 15) < 8, left, right)
    cprev = shifted(side[:, :, NY - HALO :].reshape(8, FIELDS * HALO, 128), "gy", True)
    cnext = shifted(side[:, :, :HALO].reshape(8, FIELDS * HALO, 128), "gy", False)
    return yprev, ynext, side, cprev, cnext


def in_blocks(array, dim, peers):
    before, after = (array.shape[:dim], array.shape[dim + 1 :])
    return jnp.moveaxis(array.reshape(*before, peers, -1, *after), dim, 0)


def joined_along(parts, dim):
    parts = jnp.moveaxis(parts, 0, dim)
    lengths = parts.shape
    return parts.reshape(*lengths[:dim], lengths[dim] * lengths[dim + 1], *lengths[dim + 2 :])


def copy_for_each(array, axis):
    copies = jnp.broadcast_to(array, (lax.axis_size(axis), *array.shape))
    return lax.all_to_all(copies, axis, split_axis=0, concat_axis=0, tiled=True)


def slip_part(spectra, rupture_patches, slip_weights):
    freqs = spectra.shape[1] // 2
    groups_x = lax.axis_size("gx")
    groups_y = lax.axis_size("gy")
    devices = groups_x * groups_y
    owner = lax.axis_index("gx") * groups_y + lax.axis_index("gy")
    per_dev = spectra.shape[0]
    rup_group, slot_dev, variations = slip_weights.shape
    slots = rupture_patches.shape[1]
    flat_ids = rupture_patches.reshape(-1)
    slot_index = jnp.arange(flat_ids.shape[0], dtype=jnp.int32)
    target = slot_index // slots // rup_group * groups_y + slot_index % slots // slot_dev
    own_ids = owner * per_dev + jnp.arange(per_dev, dtype=jnp.int32)
    matches = flat_ids[None, :] == own_ids[:, None]
    target_of = jnp.max(jnp.where(matches, target[None, :], -1), axis=1)
    counter = jnp.arange(per_dev, dtype=jnp.int32)
    before = counter[None, :] < counter[:, None]
    rank = jnp.sum(((target_of[None, :] == target_of[:, None]) & before).astype(jnp.int32), axis=1)
    bucket = jnp.where(target_of >= 0, target_of * CAP + rank, -1)
    placing = (jnp.arange(devices * CAP, dtype=jnp.int32)[:, None] == bucket[None, :]).astype(
        jnp.bfloat16
    )
    rounded = spectra.astype(jnp.bfloat16)
    outgoing = jnp.dot(placing, rounded, preferred_element_type=jnp.float32).astype(jnp.bfloat16)
    received = lax.all_to_all(
        outgoing.reshape(devices, CAP, 2 * freqs), ("gx", "gy"), 0, 0, tiled=True
    ).reshape(devices * CAP, 2 * freqs)
    local_ids = lax.dynamic_slice(
        rupture_patches,
        (lax.axis_index("gx") * rup_group, lax.axis_index("gy") * slot_dev),
        (rup_group, slot_dev),
    ).reshape(-1)
    source = local_ids // per_dev
    earlier_slot = (
        (local_ids[None, :] < local_ids[:, None])
        & (source[None, :] == source[:, None])
        & (local_ids[None, :] >= 0)
    )
    rank_in = jnp.sum(earlier_slot.astype(jnp.int32), axis=1)
    live = local_ids >= 0
    row = jnp.where(live, source * CAP + rank_in, 0)
    picked = jnp.take(received, row, axis=0)
    slot_spectra = jnp.where(live[:, None], picked, jnp.zeros_like(picked)).reshape(
        rup_group, slot_dev, 2 * freqs
    )
    swapped = lax.all_to_all(slip_weights, "gy", split_axis=2, concat_axis=1, tiled=True)
    return jnp.einsum(
        "rsv,rsf->rvf",
        swapped,
        joined_along(copy_for_each(slot_spectra, "gy"), 1),
        preferred_element_type=jnp.float32,
    )


def per_device(
    velocity,
    pressure,
    memory,
    buoyancy,
    modulus,
    relax,
    strength,
    spectra,
    patch_cell,
    rupture_patches,
    slip_weights,
):
    fields = (pressure, memory, buoyancy, modulus, relax, strength)
    halos = halo_exchange(velocity, fields)
    velocity, pressure, memory, spectra = four_steps(velocity, fields, spectra, patch_cell, halos)
    slip = slip_part(spectra, rupture_patches, slip_weights)
    return (velocity, pressure, memory, spectra, slip)


def solution(mesh):
    field = P(None, "gy", "gx")
    in_specs = (
        (P(None, None, "gy", "gx"),)
        + (field,) * 6
        + (P(("gx", "gy"), None), P(("gx", "gy")), P(), P("gx", "gy", None))
    )
    out_specs = (
        P(None, None, "gy", "gx"),
        field,
        field,
        P(("gx", "gy"), None),
        P("gx", "gy", None),
    )
    return jax.shard_map(
        per_device, mesh=mesh, in_specs=in_specs, out_specs=out_specs, check_vma=False
    )
```

```python
import functools

import jax
import jax.numpy as jnp
from jax import lax
from jax.experimental import pallas as pl
from jax.experimental.pallas import tpu as pltpu
from jax.sharding import PartitionSpec as P

STEPS = 4
CAP = 2
NZ, NY, NX = 64, 32, 128
HALO = 8
EY = NY + 2 * HALO
FIELDS = 9
VX, VY, VZ, PR, ME, BU, MO, RE, ST = range(FIELDS)
BP = FIELDS


def lanes(shape):
    return lax.broadcasted_iota(jnp.int32, shape, len(shape) - 1)


def roll(x, shift, axis=1):
    shift = shift % x.shape[axis]
    return pltpu.roll(x, shift, axis) if shift else x


def pack_kernel(vel, pr, me, bu, mo, re, st, lo_ref, hi_ref, q_ref):
    lane = lanes((NY, 128))
    fields = [vel.at[0], vel.at[1], vel.at[2], pr, me, bu, mo, re, st]
    for f, ref in enumerate(fields):
        lows, highs = [], []
        strip = jnp.zeros((NY, 128), jnp.float32)
        for g in range(8):
            plane = ref[g, 0]
            turned = roll(plane, 8 + 16 * g)
            strip = jnp.where((lane >> 4) == g, turned, strip)
            ends = turned[:HALO], turned[NY - HALO :]
            if f == VX:
                ends = tuple(roll(e, -1) for e in ends)
            lows.append(ends[0])
            highs.append(ends[1])
        lo_ref[0, f] = jnp.concatenate(lows, axis=0).astype(jnp.bfloat16)
        hi_ref[0, f] = jnp.concatenate(highs, axis=0).astype(jnp.bfloat16)
        q_ref[0, f] = strip.astype(jnp.bfloat16)


def pack(velocity, *fields):
    spec = pl.BlockSpec((8, 1, NY, NX), lambda i: (0, i, 0, 0))
    vspec = pl.BlockSpec((3, 8, 1, NY, NX), lambda i: (0, 0, i, 0, 0))
    yspec = pl.BlockSpec((1, FIELDS, 64, 128), lambda i: (i, 0, 0, 0))
    qspec = pl.BlockSpec((1, FIELDS, NY, 128), lambda i: (i, 0, 0, 0))
    yshape = jax.ShapeDtypeStruct((8, FIELDS, 64, 128), jnp.bfloat16)
    qshape = jax.ShapeDtypeStruct((8, FIELDS, NY, 128), jnp.bfloat16)
    return pl.pallas_call(
        pack_kernel,
        out_shape=(yshape, yshape, qshape),
        grid=(8,),
        in_specs=[vspec] + [spec] * 6,
        out_specs=(yspec, yspec, qspec),
        name="pack",
    )(velocity.reshape(3, 8, 8, NY, NX), *[f.reshape(8, 8, NY, NX) for f in fields])


def shifted(array, axis, up):
    n = lax.axis_size(axis)
    pairs = [(i, i + 1) if up else (i + 1, i) for i in range(n - 1)]
    return lax.ppermute(array, axis, pairs)


def ydiff(x):
    return roll(x, -1, 0) - roll(x, 1, 0)


def turned_diff(x, other, at):
    return roll(jnp.where(at == 8, other, x), -2) - jnp.where(at == 7, other, x)


def back_diff(x, other, at):
    return jnp.where(at == 7, other, x) - roll(jnp.where(at == 6, other, x), 2)


def steps_kernel(
    cell,
    vel,
    pr,
    me,
    bu,
    mo,
    re,
    st,
    spectra,
    phase,
    lane_of,
    yprev,
    ynext,
    side,
    cprev,
    cnext,
    vel_o,
    pr_o,
    me_o,
    spec_o,
    samp_o,
    E,
    S,
    X,
    shear,
    G,
    sems,
):
    sources = [vel.at[0], vel.at[1], vel.at[2], pr, me, bu, mo, re, st]
    copies = [
        [pltpu.make_async_copy(src.at[:, zi], X.at[f, :, zi], sems.at[f, zi]) for f, src in enumerate(sources)]
        for zi in range(8)
    ]
    for row in copies:
        for c in row:
            c.start()
    lane = lanes((EY, 128))
    lane16 = lane & 15
    group = lane >> 4
    zero = jnp.zeros((EY, 128), jnp.float32)

    def fill(zi):
        cp = cprev[zi].astype(jnp.float32)
        cn = cnext[zi].astype(jnp.float32)
        for f in range(FIELDS):
            yp = yprev[zi, f].astype(jnp.float32)
            yn = ynext[zi, f].astype(jnp.float32)
            for g in range(8):
                z = g * 10 + zi + 1
                low, high = yp[8 * g : 8 * g + 8], yn[8 * g : 8 * g + 8]
                mid = roll(X[f, g, zi], (7 if f == VX else 8) + 16 * g)
                E[f, z, :HALO] = low
                E[f, z, HALO + NY :] = high
                E[f, z, HALO : HALO + NY] = mid
                if f == BU:
                    E[BP, z, :HALO] = roll(low, -1)
                    E[BP, z, HALO + NY :] = roll(high, -1)
                    E[BP, z, HALO : HALO + NY] = roll(mid, -1)
            low, high = cp[8 * f : 8 * f + 8], cn[8 * f : 8 * f + 8]
            mid = side[zi, f].astype(jnp.float32)
            if f in (VX, BU):
                to = VX if f == VX else BP
                S[to, zi + 1, :HALO] = roll(low, -1)
                S[to, zi + 1, HALO + NY :] = roll(high, -1)
                S[to, zi + 1, HALO : HALO + NY] = roll(mid, -1)
            if f != VX:
                S[f, zi + 1, :HALO] = low
                S[f, zi + 1, HALO + NY :] = high
                S[f, zi + 1, HALO : HALO + NY] = mid

    def wrap_planes(f):
        S[f, 0] = jnp.where(lane < 16, 0.0, roll(S[f, 8], 16))
        S[f, 9] = jnp.where(lane >= 112, 0.0, roll(S[f, 1], -16))
        for g in range(8):
            E[f, 10 * g] = roll(E[f, 10 * g - 2], 16) if g else zero
            E[f, 10 * g + 9] = roll(E[f, 10 * g + 11], -16) if g < 7 else zero

    spec_o[...] = spectra[...]
    samp_o[...] = jnp.zeros_like(samp_o)
    for zi in range(8):
        for c in copies[zi]:
            c.wait()
        fill(zi)
    wrap_planes(PR)

    def moved(ref, z, dx, p):
        ref[VX, z] = ref[VX, z] - ref[BP, z] * dx
        b = ref[BU, z]
        ref[VY, z] = ref[VY, z] - b * ydiff(p)
        ref[VZ, z] = ref[VZ, z] - b * (ref[PR, z + 1] - ref[PR, z - 1])

    def velocities(zi, _):
        zs = zi + 1
        ps = S[PR, zs]
        join = zero
        for g in range(8):
            z = g * 10 + zi + 1
            p = E[PR, z]
            moved(E, z, turned_diff(p, ps, lane - 16 * g), p)
            join = jnp.where(group == g, p, join)
        moved(S, zs, turned_diff(ps, join, lane16), ps)
        return 0

    def updated(ref, z, spread):
        m = ref[ME, z]
        m = m - ref[RE, z] * (m + ref[ST, z] * spread)
        ref[ME, z] = m
        ref[PR, z] = ref[PR, z] - ref[MO, z] * (spread + m)

    def pressures(zi, _):
        zs = zi + 1
        svx, svy = S[VX, zs], S[VY, zs]
        svy_in = svy[HALO : HALO + NY]
        lane_in = lane[:NY]
        join = zero
        for g in range(8):
            z = g * 10 + zi + 1
            vx, vy = E[VX, z], E[VY, z]
            spread = back_diff(vx, svx, lane - 16 * g) + ydiff(vy)
            updated(E, z, spread + (E[VZ, z + 1] - E[VZ, z - 1]))
            row = pl.multiple_of((g * 8 + zi) * NY, NY)
            shear[pl.ds(row, NY), :] = ydiff(vx)[HALO : HALO + NY] + turned_diff(
                vy[HALO : HALO + NY], svy_in, lane_in - 16 * g
            )
            join = jnp.where(group == g, vx, join)
        spread = back_diff(svx, join, lane16) + ydiff(svy)
        updated(S, zs, spread + (S[VZ, zs + 1] - S[VZ, zs - 1]))
        return 0

    wanted = lanes((256, 128)) == lane_of[...]

    def step(n, _):
        lax.fori_loop(0, 8, velocities, 0)
        wrap_planes(VZ)
        lax.fori_loop(0, 8, pressures, 0)
        wrap_planes(PR)

        def pick(i, _):
            for k in range(8):
                c = cell[i * 8 + k]
                G[pl.ds(i * 8 + k, 1), :] = shear[pl.ds(c >> 7, 1), :]
            return 0

        lax.fori_loop(0, 32, pick, 0)
        sample = jnp.sum(jnp.where(wanted, G[...], 0.0), axis=1, keepdims=True)
        spec_o[...] = spec_o[...] + sample * phase[pl.ds(n, 1), :]
        samp_o[...] = jnp.where(lanes((256, 128)) == n, sample, samp_o[...])
        return 0

    lax.fori_loop(0, STEPS, step, 0)
    targets = [vel_o.at[0], vel_o.at[1], vel_o.at[2], pr_o, me_o]
    outs = []
    for zi in range(8):
        for f, dst in enumerate(targets):
            for g in range(8):
                plane = E[f, g * 10 + zi + 1, HALO : HALO + NY]
                X[f, g, zi] = roll(plane, -(7 if f == VX else 8) - 16 * g)
            outs.append(pltpu.make_async_copy(X.at[f, :, zi], dst.at[:, zi], sems.at[f, zi]))
            outs[-1].start()
    for c in outs:
        c.wait()


def phase_rows(freqs):
    rows = []
    for step in range(1, STEPS + 1):
        angle = jnp.pi * (jnp.arange(freqs, dtype=jnp.float32) + 0.5) / freqs * step
        rows.append(jnp.concatenate([jnp.cos(angle), -jnp.sin(angle)]))
    return jnp.stack(rows)


def four_steps(velocity, fields, spectra, patch_cell, halos):
    any_spec = pl.BlockSpec(memory_space=pl.ANY)
    vmem = pl.BlockSpec(memory_space=pltpu.VMEM)
    smem = pl.BlockSpec(memory_space=pltpu.SMEM)
    field = jax.ShapeDtypeStruct((8, 8, NY, NX), jnp.float32)
    vel, pr, me, spec, samples = pl.pallas_call(
        steps_kernel,
        out_shape=(
            jax.ShapeDtypeStruct((3, 8, 8, NY, NX), jnp.float32),
            field,
            field,
            jax.ShapeDtypeStruct(spectra.shape, jnp.float32),
            jax.ShapeDtypeStruct((spectra.shape[0], 128), jnp.float32),
        ),
        in_specs=[smem] + [any_spec] * 7 + [vmem] * 8,
        out_specs=(any_spec, any_spec, any_spec, vmem, vmem),
        scratch_shapes=[
            pltpu.VMEM((FIELDS + 1, 80, EY, 128), jnp.float32),
            pltpu.VMEM((FIELDS + 1, 10, EY, 128), jnp.float32),
            pltpu.VMEM((FIELDS, 8, 8, NY, 128), jnp.float32),
            pltpu.VMEM((NZ * NY, 128), jnp.float32),
            pltpu.VMEM((256, 128), jnp.float32),
            pltpu.SemaphoreType.DMA((FIELDS, 8)),
        ],
        compiler_params=pltpu.CompilerParams(vmem_limit_bytes=56 * 1024 * 1024),
        name="four_steps",
    )(
        patch_cell,
        velocity.reshape(3, 8, 8, NY, NX),
        *[f.reshape(8, 8, NY, NX) for f in fields],
        spectra,
        phase_rows(spectra.shape[1] // 2),
        ((patch_cell + 7 + 16 * (patch_cell >> 15)) & 127)[:, None],
        *halos,
    )
    shape = (NZ, NY, NX)
    return vel.reshape(velocity.shape), pr.reshape(shape), me.reshape(shape), spec, samples


def halo_exchange(velocity, fields):
    lo, hi, q = pack(velocity, *fields)
    yprev = shifted(hi, "gy", True)
    ynext = shifted(lo, "gy", False)
    left = shifted(q, "gx", True)
    right = shifted(q, "gx", False)
    side = jnp.where((jnp.arange(128) & 15) < 8, left, right)
    cprev = shifted(side[:, :, NY - HALO :].reshape(8, FIELDS * HALO, 128), "gy", True)
    cnext = shifted(side[:, :, :HALO].reshape(8, FIELDS * HALO, 128), "gy", False)
    return yprev, ynext, side, cprev, cnext


def rows_of(shape):
    return lax.broadcasted_iota(jnp.int32, shape, 0)


def transposed_dot(a, b):
    return lax.dot_general(a, b, (((0,), (0,)), ((), ())), preferred_element_type=jnp.float32)


def as_row(column, n):
    eye = rows_of((n, n)) == lanes((n, n))
    return jnp.sum(jnp.where(eye, column, 0.0), axis=0, keepdims=True)


def as_column(row, n):
    eye = rows_of((n, n)) == lanes((n, n))
    return jnp.sum(jnp.where(eye, row, 0.0), axis=1, keepdims=True)


def route_kernel(where, table, spectra, weights, send, place, pick, hot, turned, stage):
    n = spectra.shape[0]
    gx, gy = where[0], where[1]
    base = (gx * 16 + gy) * n
    mine = table[pl.ds(pl.multiple_of(gx * 8, 8), 8), :].astype(jnp.float32)
    mine = pltpu.roll(mine, lax.rem(512 - 32 * gy, 512), 1)[:, :128]
    quarter = lanes((1, 128)) >> 5
    halves = []
    for h in range(2):
        half = jnp.zeros((1, 128), jnp.float32)
        for q in range(4):
            r = 4 * h + q
            half = jnp.where(quarter == q, roll(mine, 32 * q)[r : r + 1], half)
        halves.append(half)
    ids_r = jnp.concatenate(halves, axis=1)
    ids = as_column(ids_r, n).astype(jnp.int32)
    ids_r = ids_r.astype(jnp.int32)
    columns = []
    for chunk in range(n // 32):
        own = base + chunk * 32 + rows_of((32, 512))

        def search(r8, found):
            for k in range(8):
                r = r8 * 8 + k
                found = jnp.where(table[pl.ds(r, 1), :] == own, r, found)
            return found

        found = lax.fori_loop(0, table.shape[0] // 8, search, jnp.full((32, 512), -1, jnp.int32))
        slot = jnp.where(found >= 0, found * 512 + lanes((32, 512)), -1).astype(jnp.float32)
        columns.append(jnp.max(slot, axis=1, keepdims=True))
    slot = jnp.concatenate(columns, axis=0).astype(jnp.int32)
    rupture = slot >> 9
    target = (((rupture >> 3) << 4) + ((slot & 511) >> 5)).astype(jnp.float32)
    hot[...] = (lanes((n, 128)) == rupture).astype(jnp.float32).astype(jnp.bfloat16)
    target_row = as_row(target, n)
    before = rows_of((n, n)) < lanes((n, n))
    rank = jnp.sum(
        jnp.where((target == target_row) & before, 1.0, 0.0), axis=0, keepdims=True
    )
    same = (ids >> 8) == (ids_r >> 8)
    rank_in = jnp.sum(jnp.where(same & (ids < ids_r), 1.0, 0.0), axis=0, keepdims=True)
    device = rows_of((128, n))
    target_row = target_row.astype(jnp.int32)
    source_row = ids_r >> 8
    stage[...] = jnp.zeros_like(stage)
    rounded = spectra[...].astype(jnp.bfloat16)
    for k in range(CAP):
        to = jnp.where((device == target_row) & (rank == k), 1.0, 0.0).astype(jnp.bfloat16)
        back = jnp.where((device == source_row) & (rank_in == k), 1.0, 0.0).astype(jnp.bfloat16)
        place[k] = to
        pick[k] = back
        sent = jnp.dot(to, rounded, preferred_element_type=jnp.float32)
        sent_w = jnp.dot(back, weights[...], preferred_element_type=jnp.float32)
        for c in range(2):
            stage[:, 6 * k + c, :] = sent[:, 128 * c : 128 * (c + 1)]
        for c in range(4):
            stage[:, 6 * k + 2 + c, :] = sent_w[:, 128 * c : 128 * (c + 1)]
    send[...] = stage[...].astype(jnp.bfloat16)
    eye = (rows_of((n, n)) == lanes((n, n))).astype(jnp.float32).astype(jnp.bfloat16)
    turned[...] = transposed_dot(weights[...], eye).astype(jnp.bfloat16).reshape(turned.shape)


def sort_kernel(received, place, pick, turned, message, patch_weights, stage):
    stage[...] = received[...].astype(jnp.float32)
    spectra = jnp.zeros((256, 256), jnp.float32)
    mine = jnp.zeros((256, 512), jnp.float32)
    for k in range(CAP):
        parts = [stage[:, 6 * k + c, :].astype(jnp.bfloat16) for c in range(6)]
        spectra += transposed_dot(pick[k], jnp.concatenate(parts[:2], axis=1))
        mine += transposed_dot(place[k], jnp.concatenate(parts[2:], axis=1))
    patch_weights[...] = mine.astype(jnp.bfloat16)
    for j in range(16):
        message[j, :256] = spectra.astype(jnp.bfloat16)
        message[j, 256:] = turned[j]


def sums_kernel(samples, hot, patch_weights, out):
    lane = lanes((256, 128))
    sums = []
    listed = hot[...].astype(jnp.float32)
    for n in range(STEPS):
        sample = jnp.sum(jnp.where(lane == n, samples[...], 0.0), axis=1, keepdims=True)
        scaled = listed * sample
        high = scaled.astype(jnp.bfloat16)
        rest = (scaled - high.astype(jnp.float32)).astype(jnp.bfloat16).astype(jnp.float32)
        both = scaled.astype(jnp.bfloat16).astype(jnp.float32) + roll(rest, 64)
        total = transposed_dot(both.astype(jnp.bfloat16), patch_weights[...])
        sums.append(total[:64] + total[64:])
    quarter = lanes((64, 128)) >> 5
    for j in range(16):
        block = slice(128 * (j // 4), 128 * (j // 4) + 128)
        packed = jnp.zeros((64, 128), jnp.float32)
        for n in range(STEPS):
            packed = jnp.where(quarter == n, roll(sums[n][:, block], 32 * (n - j % 4)), packed)
        out[:, j] = packed.reshape(8, 8, 128)


def slip_kernel(gathered, sums, phase, out):
    total = jnp.sum(sums[...], axis=0)
    own = (lanes((32, 128)) & 31) == rows_of((32, 128))
    left = jnp.concatenate(
        [jnp.where(own, total[r : r + 1], 0.0) for r in range(8)], axis=0
    )
    slip = jnp.dot(
        left, phase[...], precision=lax.Precision.HIGHEST, preferred_element_type=jnp.float32
    )
    square = (256, 256)
    same = ((rows_of(square) >> 5) == (lanes(square) >> 5)).astype(jnp.float32)
    same = same.astype(jnp.bfloat16)
    for j in range(16):
        spread = jnp.concatenate([gathered[j, 256:]] * 8, axis=0) * same
        slip += jnp.dot(spread, gathered[j, :256], preferred_element_type=jnp.float32)
    out[...] = slip.reshape(out.shape)


def small_call(kernel, outs, name, scratch=(), smem=0, inputs=0):
    vmem = pl.BlockSpec(memory_space=pltpu.VMEM)
    specs = [pl.BlockSpec(memory_space=pltpu.SMEM)] * smem + [vmem] * (inputs - smem)
    shapes = tuple(jax.ShapeDtypeStruct(s, d) for s, d in outs)
    return pl.pallas_call(
        kernel,
        out_shape=shapes,
        in_specs=specs,
        out_specs=(vmem,) * len(shapes),
        scratch_shapes=scratch,
        name=name,
    )


def routed(spectra, rupture_patches, slip_weights):
    bf16, f32 = jnp.bfloat16, jnp.float32
    where = jnp.stack([lax.axis_index("gx"), lax.axis_index("gy")])
    tiles = (128, 16, 128)
    return small_call(
        route_kernel,
        [
            (tiles, bf16),
            ((2, 128, 256), bf16),
            ((2, 128, 256), bf16),
            ((256, 128), bf16),
            ((16, 32, 256), bf16),
        ],
        "route",
        [pltpu.VMEM(tiles, f32)],
        1,
        4,
    )(where, rupture_patches, spectra, slip_weights.reshape(256, 512))


def sorted_rows(received, place, pick, turned):
    return small_call(
        sort_kernel,
        [((16, 288, 256), jnp.bfloat16), ((256, 512), jnp.bfloat16)],
        "sort",
        [pltpu.VMEM(received.shape, jnp.float32)],
        0,
        4,
    )(received, place, pick, turned)


def slip_response(gathered, patch_weights, hot, samples):
    f32 = jnp.float32
    (sums,) = small_call(sums_kernel, [((8, 16, 8, 128), f32)], "sums", (), 0, 3)(
        samples, hot, patch_weights
    )
    sums = lax.all_to_all(sums.reshape(128, 8, 128), ("gx", "gy"), 0, 0, tiled=True)
    phase = jnp.repeat(phase_rows(128), 32, axis=0)
    (slip,) = small_call(slip_kernel, [((8, 32, 256), f32)], "slip", (), 0, 3)(
        gathered, sums, phase
    )
    return slip


def per_device(
    velocity,
    pressure,
    memory,
    buoyancy,
    modulus,
    relax,
    strength,
    spectra,
    patch_cell,
    rupture_patches,
    slip_weights,
):
    fields = (pressure, memory, buoyancy, modulus, relax, strength)
    halos = halo_exchange(velocity, fields)
    send, place, pick, hot, turned = routed(spectra, rupture_patches, slip_weights)
    received = lax.all_to_all(send, ("gx", "gy"), 0, 0, tiled=True)
    received, _ = lax.optimization_barrier((received, halos))
    message, patch_weights = sorted_rows(received, place, pick, turned)
    gathered = lax.all_to_all(message, "gy", 0, 0, tiled=True)
    spectra, message = lax.optimization_barrier((spectra, message))
    velocity, pressure, memory, spectra, samples = four_steps(
        velocity, fields, spectra, patch_cell, halos
    )
    samples, gathered = lax.optimization_barrier((samples, gathered))
    slip = slip_response(gathered, patch_weights, hot, samples)
    return (velocity, pressure, memory, spectra, slip)


def solution(mesh):
    field = P(None, "gy", "gx")
    in_specs = (
        (P(None, None, "gy", "gx"),)
        + (field,) * 6
        + (P(("gx", "gy"), None), P(("gx", "gy")), P(), P("gx", "gy", None))
    )
    out_specs = (
        P(None, None, "gy", "gx"),
        field,
        field,
        P(("gx", "gy"), None),
        P("gx", "gy", None),
    )
    return jax.shard_map(
        per_device, mesh=mesh, in_specs=in_specs, out_specs=out_specs, check_vma=False
    )
```

```python
import jax
import jax.numpy as jnp
import numpy as np
from jax import lax
from jax.experimental import pallas as pl
from jax.experimental.pallas import tpu as pltpu
from jax.sharding import PartitionSpec as P

STEPS = 4
CAP = 2
NZ, NY, NX = 64, 32, 128
HALO = 8
EY = NY + 2 * HALO
FIELDS = 9
VX, VY, VZ, PR, ME, BU, MO, RE, ST = range(FIELDS)
BP = FIELDS
REACH = [7, 7, 6, 8, 6, 7, 6, 6, 6]
SENT = [(f, d) for f in range(FIELDS) for d in range(REACH[f])]
ROWS = 8 * (len(SENT) + len(SENT) % 2)


def lanes(shape):
    return lax.broadcasted_iota(jnp.int32, shape, len(shape) - 1)


def roll(x, shift, axis=1):
    shift = shift % x.shape[axis]
    return pltpu.roll(x, shift, axis) if shift else x


def pack_kernel(vel, pr, me, bu, mo, re, st, lo_ref, hi_ref, q_ref, lows, highs):
    lane = lanes((NY, 128))
    fields = [vel.at[0], vel.at[1], vel.at[2], pr, me, bu, mo, re, st]
    for f, ref in enumerate(fields):
        strip = jnp.zeros((NY, 128), jnp.float32)
        for g in range(8):
            turned = roll(ref[g, 0], 8 + 16 * g)
            strip = jnp.where((lane >> 4) == g, turned, strip)
            low, high = turned[:HALO], turned[NY - HALO :]
            if f == VX:
                low, high = roll(low, -1), roll(high, -1)
            lows[f, pl.ds(8 * g, 8)] = low
            highs[f, pl.ds(8 * g, 8)] = high
        q_ref[0, f] = strip.astype(jnp.bfloat16)
    for ref, ends, first in ((lo_ref, lows, False), (hi_ref, highs, True)):
        tiles = [
            ends[f, pl.ds(d + (HALO - REACH[f] if first else 0), 8, stride=8)] for f, d in SENT
        ]
        if len(tiles) % 2:
            tiles.append(tiles[-1])
        for t in range(0, len(tiles), 2):
            pair = jnp.concatenate(tiles[t : t + 2], axis=0)
            ref[0, pl.ds(8 * t, 16)] = pair.astype(jnp.bfloat16)


def pack(velocity, *fields):
    spec = pl.BlockSpec((8, 1, NY, NX), lambda i: (0, i, 0, 0))
    vspec = pl.BlockSpec((3, 8, 1, NY, NX), lambda i: (0, 0, i, 0, 0))
    yspec = pl.BlockSpec((1, ROWS, 128), lambda i: (i, 0, 0))
    qspec = pl.BlockSpec((1, FIELDS, NY, 128), lambda i: (i, 0, 0, 0))
    yshape = jax.ShapeDtypeStruct((8, ROWS, 128), jnp.bfloat16)
    qshape = jax.ShapeDtypeStruct((8, FIELDS, NY, 128), jnp.bfloat16)
    return pl.pallas_call(
        pack_kernel,
        out_shape=(yshape, yshape, qshape),
        grid=(8,),
        in_specs=[vspec] + [spec] * 6,
        out_specs=(yspec, yspec, qspec),
        scratch_shapes=[pltpu.VMEM((FIELDS, 64, 128), jnp.float32)] * 2,
        name="pack",
    )(velocity.reshape(3, 8, 8, NY, NX), *[f.reshape(8, 8, NY, NX) for f in fields])


def shifted(array, axis, up):
    n = lax.axis_size(axis)
    pairs = [(i, i + 1) if up else (i + 1, i) for i in range(n - 1)]
    return lax.ppermute(array, axis, pairs)


def ydiff(x):
    return roll(x, -1, 0) - roll(x, 1, 0)


def turned_diff(x, other, at):
    return roll(jnp.where(at == 8, other, x), -2) - jnp.where(at == 7, other, x)


def back_diff(x, other, at):
    return jnp.where(at == 7, other, x) - roll(jnp.where(at == 6, other, x), 2)


def steps_kernel(
    cell,
    vel,
    pr,
    me,
    bu,
    mo,
    re,
    st,
    spectra,
    phase,
    hot,
    patch_weights,
    yprev,
    ynext,
    side,
    cprev,
    cnext,
    vel_o,
    pr_o,
    me_o,
    spec_o,
    sums_o,
    E,
    S,
    X,
    T,
    shear,
    G,
    L,
    sems,
):
    sources = [vel.at[0], vel.at[1], vel.at[2], pr, me, bu, mo, re, st]
    copies = [
        [pltpu.make_async_copy(src.at[:, zi], X.at[f, :, zi], sems.at[f, zi]) for f, src in enumerate(sources)]
        for zi in range(8)
    ]
    for row in copies:
        for c in row:
            c.start()
    lane = lanes((EY, 128))
    lane16 = lane & 15
    group = lane >> 4
    zero = jnp.zeros((EY, 128), jnp.float32)

    def fill(zi):
        cp = cprev[zi].astype(jnp.float32)
        cn = cnext[zi].astype(jnp.float32)
        for ref, ends, first in ((ynext, T.at[0], False), (yprev, T.at[1], True)):
            for t in range(0, len(SENT), 2):
                pair = ref[zi, pl.ds(8 * t, 16)].astype(jnp.float32)
                for k, (f, d) in enumerate(SENT[t : t + 2]):
                    at = d + (HALO - REACH[f] if first else 0)
                    ends[f, pl.ds(at, 8, stride=8)] = pair[8 * k : 8 * k + 8]
        for f in range(FIELDS):
            for g in range(8):
                z = g * 10 + zi + 1
                low, high = T[1, f, pl.ds(8 * g, 8)], T[0, f, pl.ds(8 * g, 8)]
                mid = roll(X[f, g, zi], (7 if f == VX else 8) + 16 * g)
                E[f, z, :HALO] = low
                E[f, z, HALO + NY :] = high
                E[f, z, HALO : HALO + NY] = mid
                if f == BU:
                    E[BP, z, :HALO] = roll(low, -1)
                    E[BP, z, HALO + NY :] = roll(high, -1)
                    E[BP, z, HALO : HALO + NY] = roll(mid, -1)
            low, high = cp[8 * f : 8 * f + 8], cn[8 * f : 8 * f + 8]
            mid = side[zi, f].astype(jnp.float32)
            if f in (VX, BU):
                to = VX if f == VX else BP
                S[to, zi + 1, :HALO] = roll(low, -1)
                S[to, zi + 1, HALO + NY :] = roll(high, -1)
                S[to, zi + 1, HALO : HALO + NY] = roll(mid, -1)
            if f != VX:
                S[f, zi + 1, :HALO] = low
                S[f, zi + 1, HALO + NY :] = high
                S[f, zi + 1, HALO : HALO + NY] = mid

    def wrap_planes(f):
        S[f, 0] = jnp.where(lane < 16, 0.0, roll(S[f, 8], 16))
        S[f, 9] = jnp.where(lane >= 112, 0.0, roll(S[f, 1], -16))
        for g in range(8):
            E[f, 10 * g] = roll(E[f, 10 * g - 2], 16) if g else zero
            E[f, 10 * g + 9] = roll(E[f, 10 * g + 11], -16) if g < 7 else zero

    T[...] = jnp.zeros_like(T)
    for zi in range(8):
        for c in copies[zi]:
            c.wait()
        fill(zi)
    wrap_planes(PR)

    def moved(ref, z, dx, p):
        ref[VX, z] = ref[VX, z] - ref[BP, z] * dx
        b = ref[BU, z]
        ref[VY, z] = ref[VY, z] - b * ydiff(p)
        ref[VZ, z] = ref[VZ, z] - b * (ref[PR, z + 1] - ref[PR, z - 1])

    def velocities(zi):
        zs = zi + 1
        ps = S[PR, zs]
        join = zero
        for g in range(8):
            z = g * 10 + zi + 1
            p = E[PR, z]
            moved(E, z, turned_diff(p, ps, lane - 16 * g), p)
            join = jnp.where(group == g, p, join)
        moved(S, zs, turned_diff(ps, join, lane16), ps)

    def updated(ref, z, spread, rows):
        m = ref[ME, z, rows]
        m = m - ref[RE, z, rows] * (m + ref[ST, z, rows] * spread)
        ref[ME, z, rows] = m
        ref[PR, z, rows] = ref[PR, z, rows] - ref[MO, z, rows] * (spread + m)

    def pressures(n, last, zi):
        zs = zi + 1
        rows = slice(HALO, HALO + NY) if last else slice(0, EY)
        svx, svy = S[VX, zs], S[VY, zs]
        svy_in = svy[HALO : HALO + NY]
        lane_in = lane[:NY]
        join = zero
        for g in range(8):
            z = g * 10 + zi + 1
            vx, vy = E[VX, z], E[VY, z]
            spread = back_diff(vx[rows], svx[rows], lane[rows] - 16 * g) + ydiff(vy)[rows]
            updated(E, z, spread + (E[VZ, z + 1, rows] - E[VZ, z - 1, rows]), rows)
            row = pl.multiple_of((n * NZ + g * 8 + zi) * NY, NY)
            shear[pl.ds(row, NY), :] = ydiff(vx)[HALO : HALO + NY] + turned_diff(
                vy[HALO : HALO + NY], svy_in, lane_in - 16 * g
            )
            if not last:
                join = jnp.where(group == g, vx, join)
        if not last:
            spread = back_diff(svx, join, lane16) + ydiff(svy)
            updated(S, zs, spread + (S[VZ, zs + 1] - S[VZ, zs - 1]), rows)

    def looped(body):
        def one(zi, _):
            body(zi)
            return 0

        lax.fori_loop(0, 8, one, 0)

    def step(n, last):
        looped(velocities)
        wrap_planes(VZ)
        looped(lambda zi: pressures(n, last, zi))
        if not last:
            wrap_planes(PR)
        return 0

    lax.fori_loop(0, STEPS - 1, lambda n, _: step(n, False), 0)
    step(STEPS - 1, True)
    targets = [vel_o.at[0], vel_o.at[1], vel_o.at[2], pr_o, me_o]
    outs = []
    for zi in range(8):
        for f, dst in enumerate(targets):
            for g in range(8):
                plane = E[f, g * 10 + zi + 1, HALO : HALO + NY]
                X[f, g, zi] = roll(plane, -(7 if f == VX else 8) - 16 * g)
            outs.append(pltpu.make_async_copy(X.at[f, :, zi], dst.at[:, zi], sems.at[f, zi]))
            outs[-1].start()

    def pick(i, _):
        for k in range(8):
            at = i * 8 + k
            c = cell[at]
            for n in range(STEPS):
                G[n, pl.ds(at, 1), :] = shear[pl.ds(n * NZ * NY + (c >> 7), 1), :]
            L[pl.ds(at, 1), :] = jnp.full((1, 128), (c + 7 + 16 * (c >> 15)) & 127, jnp.int32)
        return 0

    lax.fori_loop(0, 32, pick, 0)
    wanted = lanes((256, 128)) == L[...]
    listed = hot[...].astype(jnp.float32)
    spec = spectra[...]
    sums = []
    for n in range(STEPS):
        sample = jnp.sum(jnp.where(wanted, G[n], 0.0), axis=1, keepdims=True)
        spec = spec + sample * phase[n : n + 1, :]
        scaled = listed * sample
        high = scaled.astype(jnp.bfloat16).astype(jnp.float32)
        both = high + roll(scaled - high, 64)
        total = transposed_dot(both.astype(jnp.bfloat16), patch_weights[...])
        sums.append(total[:64] + total[64:])
    spec_o[...] = spec
    quarter = lanes((64, 128)) >> 5
    for j in range(16):
        block = slice(128 * (j // 4), 128 * (j // 4) + 128)
        packed = jnp.zeros((64, 128), jnp.float32)
        for n in range(STEPS):
            packed = jnp.where(quarter == n, roll(sums[n][:, block], 32 * (n - j % 4)), packed)
        sums_o[:, j] = packed.reshape(8, 8, 128)
    for c in outs:
        c.wait()


def phase_rows(freqs):
    angle = np.pi * (np.arange(freqs) + 0.5) / freqs * np.arange(1, STEPS + 1)[:, None]
    return np.concatenate([np.cos(angle), -np.sin(angle)], axis=1).astype(np.float32)


def four_steps(velocity, fields, spectra, patch_cell, hot, patch_weights, halos):
    any_spec = pl.BlockSpec(memory_space=pl.ANY)
    vmem = pl.BlockSpec(memory_space=pltpu.VMEM)
    smem = pl.BlockSpec(memory_space=pltpu.SMEM)
    field = jax.ShapeDtypeStruct((8, 8, NY, NX), jnp.float32)
    vel, pr, me, spec, sums = pl.pallas_call(
        steps_kernel,
        out_shape=(
            jax.ShapeDtypeStruct((3, 8, 8, NY, NX), jnp.float32),
            field,
            field,
            jax.ShapeDtypeStruct(spectra.shape, jnp.float32),
            jax.ShapeDtypeStruct((8, 16, 8, 128), jnp.float32),
        ),
        in_specs=[smem] + [any_spec] * 7 + [vmem] * 9,
        out_specs=(any_spec, any_spec, any_spec, vmem, vmem),
        scratch_shapes=[
            pltpu.VMEM((FIELDS + 1, 80, EY, 128), jnp.float32),
            pltpu.VMEM((FIELDS + 1, 10, EY, 128), jnp.float32),
            pltpu.VMEM((FIELDS, 8, 8, NY, 128), jnp.float32),
            pltpu.VMEM((2, FIELDS, 64, 128), jnp.float32),
            pltpu.VMEM((STEPS * NZ * NY, 128), jnp.float32),
            pltpu.VMEM((STEPS, 256, 128), jnp.float32),
            pltpu.VMEM((256, 128), jnp.int32),
            pltpu.SemaphoreType.DMA((FIELDS, 8)),
        ],
        compiler_params=pltpu.CompilerParams(vmem_limit_bytes=56 * 1024 * 1024),
        name="four_steps",
    )(
        patch_cell,
        velocity.reshape(3, 8, 8, NY, NX),
        *[f.reshape(8, 8, NY, NX) for f in fields],
        spectra,
        jnp.asarray(phase_rows(spectra.shape[1] // 2)),
        hot,
        patch_weights,
        *halos,
    )
    shape = (NZ, NY, NX)
    return vel.reshape(velocity.shape), pr.reshape(shape), me.reshape(shape), spec, sums


def join_kernel(left, right, side, low, high):
    from_left = (lanes((NY, 128)) & 15) < 8
    for zi in range(8):
        lows, highs = [], []
        for f in range(FIELDS):
            strip = jnp.where(
                from_left, left[zi, f].astype(jnp.float32), right[zi, f].astype(jnp.float32)
            )
            side[zi, f] = strip.astype(jnp.bfloat16)
            lows.append(strip[:HALO])
            highs.append(strip[NY - HALO :])
        low[zi] = jnp.concatenate(lows, axis=0).astype(jnp.bfloat16)
        high[zi] = jnp.concatenate(highs, axis=0).astype(jnp.bfloat16)


def halo_exchange(velocity, fields):
    lo, hi, q = pack(velocity, *fields)
    yprev = shifted(hi, "gy", True)
    ynext = shifted(lo, "gy", False)
    left = shifted(q, "gx", True)
    right = shifted(q, "gx", False)
    side, low, high = small_call(
        join_kernel,
        [(q.shape, jnp.bfloat16)] + [((8, FIELDS * HALO, 128), jnp.bfloat16)] * 2,
        "join",
        (),
        0,
        2,
    )(left, right)
    cprev = shifted(high, "gy", True)
    cnext = shifted(low, "gy", False)
    return yprev, ynext, side, cprev, cnext


def rows_of(shape):
    return lax.broadcasted_iota(jnp.int32, shape, 0)


def transposed_dot(a, b):
    return lax.dot_general(a, b, (((0,), (0,)), ((), ())), preferred_element_type=jnp.float32)


def as_row(column, n):
    eye = rows_of((n, n)) == lanes((n, n))
    return jnp.sum(jnp.where(eye, column, 0.0), axis=0, keepdims=True)


def as_column(row, n):
    eye = rows_of((n, n)) == lanes((n, n))
    return jnp.sum(jnp.where(eye, row, 0.0), axis=1, keepdims=True)


def route_kernel(table, spectra, weights, send, place, pick, hot, turned, stage):
    n = spectra.shape[0]
    gx, gy = lax.axis_index("gx"), lax.axis_index("gy")
    base = (gx * 16 + gy) * n
    mine = table[pl.ds(pl.multiple_of(gx * 8, 8), 8), :].astype(jnp.float32)
    mine = pltpu.roll(mine, lax.rem(512 - 32 * gy, 512), 1)[:, :128]
    quarter = lanes((1, 128)) >> 5
    halves = []
    for h in range(2):
        half = jnp.zeros((1, 128), jnp.float32)
        for q in range(4):
            r = 4 * h + q
            half = jnp.where(quarter == q, roll(mine, 32 * q)[r : r + 1], half)
        halves.append(half)
    ids_r = jnp.concatenate(halves, axis=1)
    ids = as_column(ids_r, n).astype(jnp.int32)
    ids_r = ids_r.astype(jnp.int32)
    columns = []
    for chunk in range(n // 32):
        own = base + chunk * 32 + rows_of((32, 512))

        def search(r8, found):
            for k in range(8):
                r = r8 * 8 + k
                found = jnp.where(table[pl.ds(r, 1), :] == own, r, found)
            return found

        found = lax.fori_loop(0, table.shape[0] // 8, search, jnp.full((32, 512), -1, jnp.int32))
        slot = jnp.where(found >= 0, found * 512 + lanes((32, 512)), -1).astype(jnp.float32)
        columns.append(jnp.max(slot, axis=1, keepdims=True))
    slot = jnp.concatenate(columns, axis=0).astype(jnp.int32)
    rupture = slot >> 9
    target = (((rupture >> 3) << 4) + ((slot & 511) >> 5)).astype(jnp.float32)
    hot[...] = (lanes((n, 128)) == rupture).astype(jnp.float32).astype(jnp.bfloat16)
    target_row = as_row(target, n)
    before = rows_of((n, n)) < lanes((n, n))
    rank = jnp.sum(
        jnp.where((target == target_row) & before, 1.0, 0.0), axis=0, keepdims=True
    )
    same = (ids >> 8) == (ids_r >> 8)
    rank_in = jnp.sum(jnp.where(same & (ids < ids_r), 1.0, 0.0), axis=0, keepdims=True)
    device = rows_of((128, n))
    target_row = target_row.astype(jnp.int32)
    source_row = ids_r >> 8
    stage[...] = jnp.zeros_like(stage)
    rounded = spectra[...].astype(jnp.bfloat16)
    for k in range(CAP):
        to = jnp.where((device == target_row) & (rank == k), 1.0, 0.0).astype(jnp.bfloat16)
        back = jnp.where((device == source_row) & (rank_in == k), 1.0, 0.0).astype(jnp.bfloat16)
        place[k] = to
        pick[k] = back
        sent = jnp.dot(to, rounded, preferred_element_type=jnp.float32)
        sent_w = jnp.dot(back, weights[...], preferred_element_type=jnp.float32)
        for c in range(2):
            stage[:, 6 * k + c, :] = sent[:, 128 * c : 128 * (c + 1)]
        for c in range(4):
            stage[:, 6 * k + 2 + c, :] = sent_w[:, 128 * c : 128 * (c + 1)]
    send[...] = stage[...].astype(jnp.bfloat16)
    eye = (rows_of((n, n)) == lanes((n, n))).astype(jnp.float32).astype(jnp.bfloat16)
    turned[...] = transposed_dot(weights[...], eye).astype(jnp.bfloat16).reshape(turned.shape)


def sort_kernel(received, place, pick, turned, message, patch_weights, stage):
    stage[...] = received[...].astype(jnp.float32)
    spectra = jnp.zeros((256, 256), jnp.float32)
    mine = jnp.zeros((256, 512), jnp.float32)
    for k in range(CAP):
        parts = [stage[:, 6 * k + c, :].astype(jnp.bfloat16) for c in range(6)]
        spectra += transposed_dot(pick[k], jnp.concatenate(parts[:2], axis=1))
        mine += transposed_dot(place[k], jnp.concatenate(parts[2:], axis=1))
    patch_weights[...] = mine.astype(jnp.bfloat16)
    for j in range(16):
        message[j, :256] = spectra.astype(jnp.bfloat16)
        message[j, 256:] = turned[j]


def product_kernel(gathered, out):
    square = (256, 256)
    same = ((rows_of(square) >> 5) == (lanes(square) >> 5)).astype(jnp.float32)
    same = same.astype(jnp.bfloat16)
    total = jnp.zeros(square, jnp.float32)
    for j in range(16):
        spread = jnp.concatenate([gathered[j, 256:]] * 8, axis=0) * same
        total += jnp.dot(spread, gathered[j, :256], preferred_element_type=jnp.float32)
    out[...] = total


def slip_kernel(product, sums, phase, out):
    total = jnp.sum(sums[...], axis=0)
    own = (lanes((32, 128)) & 31) == rows_of((32, 128))
    left = jnp.concatenate(
        [jnp.where(own, total[r : r + 1], 0.0) for r in range(8)], axis=0
    )
    added = jnp.dot(
        left, phase[...], precision=lax.Precision.HIGHEST, preferred_element_type=jnp.float32
    )
    out[...] = (product[...] + added).reshape(out.shape)


def small_call(kernel, outs, name, scratch=(), smem=0, inputs=0):
    vmem = pl.BlockSpec(memory_space=pltpu.VMEM)
    specs = [pl.BlockSpec(memory_space=pltpu.SMEM)] * smem + [vmem] * (inputs - smem)
    shapes = tuple(jax.ShapeDtypeStruct(s, d) for s, d in outs)
    return pl.pallas_call(
        kernel,
        out_shape=shapes,
        in_specs=specs,
        out_specs=(vmem,) * len(shapes),
        scratch_shapes=scratch,
        name=name,
    )


def routed(spectra, rupture_patches, slip_weights):
    bf16, f32 = jnp.bfloat16, jnp.float32
    tiles = (128, 16, 128)
    return small_call(
        route_kernel,
        [
            (tiles, bf16),
            ((2, 128, 256), bf16),
            ((2, 128, 256), bf16),
            ((256, 128), bf16),
            ((16, 32, 256), bf16),
        ],
        "route",
        [pltpu.VMEM(tiles, f32)],
        0,
        3,
    )(rupture_patches, spectra, slip_weights.reshape(256, 512))


def sorted_rows(received, place, pick, turned):
    return small_call(
        sort_kernel,
        [((16, 288, 256), jnp.bfloat16), ((256, 512), jnp.bfloat16)],
        "sort",
        [pltpu.VMEM(received.shape, jnp.float32)],
        0,
        4,
    )(received, place, pick, turned)


def slip_response(gathered, sums):
    f32 = jnp.float32
    sums, gathered = lax.optimization_barrier((sums, gathered))
    sums = lax.all_to_all(sums.reshape(128, 8, 128), ("gx", "gy"), 0, 0, tiled=True)
    (product,) = small_call(product_kernel, [((256, 256), f32)], "product", (), 0, 1)(gathered)
    phase = jnp.asarray(np.repeat(phase_rows(128), 32, axis=0))
    (slip,) = small_call(slip_kernel, [((8, 32, 256), f32)], "slip", (), 0, 3)(
        product, sums, phase
    )
    return slip


def per_device(
    velocity,
    pressure,
    memory,
    buoyancy,
    modulus,
    relax,
    strength,
    spectra,
    patch_cell,
    rupture_patches,
    slip_weights,
):
    fields = (pressure, memory, buoyancy, modulus, relax, strength)
    halos = halo_exchange(velocity, fields)
    send, place, pick, hot, turned = routed(spectra, rupture_patches, slip_weights)
    received = lax.all_to_all(send, ("gx", "gy"), 0, 0, tiled=True)
    received, _ = lax.optimization_barrier((received, halos))
    message, patch_weights = sorted_rows(received, place, pick, turned)
    gathered = lax.all_to_all(message, "gy", 0, 0, tiled=True)
    spectra, message = lax.optimization_barrier((spectra, message))
    velocity, pressure, memory, spectra, sums = four_steps(
        velocity, fields, spectra, patch_cell, hot, patch_weights, halos
    )
    slip = slip_response(gathered, sums)
    return (velocity, pressure, memory, spectra, slip)


def solution(mesh):
    field = P(None, "gy", "gx")
    in_specs = (
        (P(None, None, "gy", "gx"),)
        + (field,) * 6
        + (P(("gx", "gy"), None), P(("gx", "gy")), P(), P("gx", "gy", None))
    )
    out_specs = (
        P(None, None, "gy", "gx"),
        field,
        field,
        P(("gx", "gy"), None),
        P("gx", "gy", None),
    )
    return jax.shard_map(
        per_device, mesh=mesh, in_specs=in_specs, out_specs=out_specs, check_vma=False
    )
```

```python
import jax
import jax.numpy as jnp
import numpy as np
from jax import lax
from jax.experimental import pallas as pl
from jax.experimental.pallas import tpu as pltpu
from jax.sharding import PartitionSpec as P

STEPS = 4
CAP = 2
NZ, NY, NX = 64, 32, 128
HALO = 8
EY = NY + 2 * HALO
FIELDS = 9
VX, VY, VZ, PR, ME, BU, MO, RE, ST = range(FIELDS)
BP = FIELDS
AHEAD = 6
REACH = [7, 7, 6, 8, 6, 7, 6, 6, 6]
SENT = [(f, d) for f in range(FIELDS) for d in range(REACH[f])]
ROWS = 8 * (len(SENT) + len(SENT) % 2)


def lanes(shape):
    return lax.broadcasted_iota(jnp.int32, shape, len(shape) - 1)


def roll(x, shift, axis=1):
    shift = shift % x.shape[axis]
    return pltpu.roll(x, shift, axis) if shift else x


def pack_kernel(
    vel, pr, me, bu, mo, re, st, turn, lo_o, hi_o, q_o, X, lo_s, hi_s, q_s, lows, highs, sems, done
):
    sources = [vel.at[0], vel.at[1], vel.at[2], pr, me, bu, mo, re, st]

    def fetch(zi):
        return [
            pltpu.make_async_copy(src.at[:, zi], X.at[f, :, zi], sems.at[f, zi])
            for f, src in enumerate(sources)
        ]

    def put(zi):
        return [
            pltpu.make_async_copy(src.at[zi], dst.at[zi], done.at[k, zi])
            for k, (src, dst) in enumerate(((lo_s, lo_o), (hi_s, hi_o), (q_s, q_o)))
        ]

    for zi in range(AHEAD):
        for c in fetch(zi):
            c.start()
    lane = lanes((NY, 128))

    def one(zi, _):
        @pl.when(zi + AHEAD < 8)
        def _():
            for c in fetch(zi + AHEAD):
                c.start()

        copies = fetch(zi)
        for c in copies:
            c.wait()
        strips = jnp.zeros((FIELDS * NY, 128), jnp.float32)
        for g in range(8):
            planes = [X[f, g, zi] for f in range(FIELDS)]
            for f, plane in enumerate(planes):
                shift = (7 if f == VX else 8) + 16 * g
                lows[f, pl.ds(8 * g, 8)] = roll(plane[:HALO], shift)
                highs[f, pl.ds(8 * g, 8)] = roll(plane[NY - HALO :], shift)
            planes = jnp.concatenate(planes, axis=0).astype(jnp.bfloat16)
            strips += jnp.dot(planes, turn[g], preferred_element_type=jnp.float32)
        q_s[zi] = strips.astype(jnp.bfloat16).reshape(FIELDS, NY, 128)
        for ref, ends, first in ((lo_s, lows, False), (hi_s, highs, True)):
            tiles = [
                ends[f, pl.ds(d + (HALO - REACH[f] if first else 0), 8, stride=8)]
                for f, d in SENT
            ]
            if len(tiles) % 2:
                tiles.append(tiles[-1])
            for t in range(0, len(tiles), 2):
                pair = jnp.concatenate(tiles[t : t + 2], axis=0)
                ref[zi, pl.ds(8 * t, 16)] = pair.astype(jnp.bfloat16)
        for c in put(zi):
            c.start()
        return 0

    lax.fori_loop(0, 8, one, 0)
    for zi in range(8):
        for c in put(zi):
            c.wait()


def pack(velocity, *fields):
    lane = np.arange(128)
    turn = np.zeros((8, 128, 128), np.float32)
    for g in range(8):
        own = lane[lane >> 4 == g]
        turn[g, (own - 8 - 16 * g) % 128, own] = 1
    any_spec = pl.BlockSpec(memory_space=pl.ANY)
    yshape, qshape = (8, ROWS, 128), (8, FIELDS, NY, 128)
    return pl.pallas_call(
        pack_kernel,
        out_shape=tuple(jax.ShapeDtypeStruct(s, jnp.bfloat16) for s in (yshape, yshape, qshape)),
        in_specs=[any_spec] * 7 + [pl.BlockSpec(memory_space=pltpu.VMEM)],
        out_specs=(any_spec,) * 3,
        scratch_shapes=[
            pltpu.VMEM((FIELDS, 8, 8, NY, 128), jnp.float32),
            pltpu.VMEM(yshape, jnp.bfloat16),
            pltpu.VMEM(yshape, jnp.bfloat16),
            pltpu.VMEM(qshape, jnp.bfloat16),
            pltpu.VMEM((FIELDS, 64, 128), jnp.float32),
            pltpu.VMEM((FIELDS, 64, 128), jnp.float32),
            pltpu.SemaphoreType.DMA((FIELDS, 8)),
            pltpu.SemaphoreType.DMA((3, 8)),
        ],
        compiler_params=pltpu.CompilerParams(vmem_limit_bytes=56 * 1024 * 1024),
        name="pack",
    )(
        velocity.reshape(3, 8, 8, NY, NX),
        *[f.reshape(8, 8, NY, NX) for f in fields],
        jnp.asarray(turn, jnp.bfloat16),
    )


def shifted(array, axis, up):
    n = lax.axis_size(axis)
    pairs = [(i, i + 1) if up else (i + 1, i) for i in range(n - 1)]
    return lax.ppermute(array, axis, pairs)


def ydiff(x):
    return roll(x, -1, 0) - roll(x, 1, 0)


def turned_diff(x, other, at):
    return roll(jnp.where(at == 8, other, x), -2) - jnp.where(at == 7, other, x)


def back_diff(x, other, at):
    return jnp.where(at == 7, other, x) - roll(jnp.where(at == 6, other, x), 2)


def steps_kernel(
    cell,
    vel,
    pr,
    me,
    bu,
    mo,
    re,
    st,
    spectra,
    phase,
    hot,
    patch_weights,
    yprev,
    ynext,
    side,
    cprev,
    cnext,
    vel_o,
    pr_o,
    me_o,
    spec_o,
    sums_o,
    E,
    S,
    X,
    T,
    shear,
    G,
    L,
    sems,
):
    sources = [vel.at[0], vel.at[1], vel.at[2], pr, me, bu, mo, re, st]

    def fetch(zi):
        return [
            pltpu.make_async_copy(src.at[:, zi], X.at[f, :, zi], sems.at[f, zi])
            for f, src in enumerate(sources)
        ]

    for zi in range(AHEAD):
        for c in fetch(zi):
            c.start()
    lane = lanes((EY, 128))
    lane16 = lane & 15
    group = lane >> 4
    zero = jnp.zeros((EY, 128), jnp.float32)

    def fill(zi):
        cp = cprev[zi].astype(jnp.float32)
        cn = cnext[zi].astype(jnp.float32)
        for ref, ends, first in ((ynext, T.at[0], False), (yprev, T.at[1], True)):
            for t in range(0, len(SENT), 2):
                pair = ref[zi, pl.ds(8 * t, 16)].astype(jnp.float32)
                for k, (f, d) in enumerate(SENT[t : t + 2]):
                    at = d + (HALO - REACH[f] if first else 0)
                    ends[f, pl.ds(at, 8, stride=8)] = pair[8 * k : 8 * k + 8]
        for f in range(FIELDS):
            for g in range(8):
                z = g * 10 + zi + 1
                low, high = T[1, f, pl.ds(8 * g, 8)], T[0, f, pl.ds(8 * g, 8)]
                mid = roll(X[f, g, zi], (7 if f == VX else 8) + 16 * g)
                E[f, z, :HALO] = low
                E[f, z, HALO + NY :] = high
                E[f, z, HALO : HALO + NY] = mid
                if f == BU:
                    E[BP, z, :HALO] = roll(low, -1)
                    E[BP, z, HALO + NY :] = roll(high, -1)
                    E[BP, z, HALO : HALO + NY] = roll(mid, -1)
            low, high = cp[8 * f : 8 * f + 8], cn[8 * f : 8 * f + 8]
            mid = side[zi, f].astype(jnp.float32)
            if f in (VX, BU):
                to = VX if f == VX else BP
                S[to, zi + 1, :HALO] = roll(low, -1)
                S[to, zi + 1, HALO + NY :] = roll(high, -1)
                S[to, zi + 1, HALO : HALO + NY] = roll(mid, -1)
            if f != VX:
                S[f, zi + 1, :HALO] = low
                S[f, zi + 1, HALO + NY :] = high
                S[f, zi + 1, HALO : HALO + NY] = mid

    def wrap_planes(f):
        S[f, 0] = jnp.where(lane < 16, 0.0, roll(S[f, 8], 16))
        S[f, 9] = jnp.where(lane >= 112, 0.0, roll(S[f, 1], -16))
        for g in range(8):
            E[f, 10 * g] = roll(E[f, 10 * g - 2], 16) if g else zero
            E[f, 10 * g + 9] = roll(E[f, 10 * g + 11], -16) if g < 7 else zero

    T[...] = jnp.zeros_like(T)
    def load(zi, _):
        @pl.when(zi + AHEAD < 8)
        def _():
            for c in fetch(zi + AHEAD):
                c.start()

        for c in fetch(zi):
            c.wait()
        fill(zi)
        return 0

    lax.fori_loop(0, 8, load, 0)
    wrap_planes(PR)

    def moved(ref, z, dx, p):
        ref[VX, z] = ref[VX, z] - ref[BP, z] * dx
        b = ref[BU, z]
        ref[VY, z] = ref[VY, z] - b * ydiff(p)
        ref[VZ, z] = ref[VZ, z] - b * (ref[PR, z + 1] - ref[PR, z - 1])

    def velocities(zi):
        zs = zi + 1
        ps = S[PR, zs]
        join = zero
        for g in range(8):
            z = g * 10 + zi + 1
            p = E[PR, z]
            moved(E, z, turned_diff(p, ps, lane - 16 * g), p)
            join = jnp.where(group == g, p, join)
        moved(S, zs, turned_diff(ps, join, lane16), ps)

    def updated(ref, z, spread, rows):
        m = ref[ME, z, rows]
        m = m - ref[RE, z, rows] * (m + ref[ST, z, rows] * spread)
        ref[ME, z, rows] = m
        ref[PR, z, rows] = ref[PR, z, rows] - ref[MO, z, rows] * (spread + m)

    def pressures(n, last, zi):
        zs = zi + 1
        rows = slice(HALO, HALO + NY) if last else slice(0, EY)
        svx, svy = S[VX, zs], S[VY, zs]
        svy_in = svy[HALO : HALO + NY]
        lane_in = lane[:NY]
        join = zero
        for g in range(8):
            z = g * 10 + zi + 1
            vx, vy = E[VX, z], E[VY, z]
            spread = back_diff(vx[rows], svx[rows], lane[rows] - 16 * g) + ydiff(vy)[rows]
            updated(E, z, spread + (E[VZ, z + 1, rows] - E[VZ, z - 1, rows]), rows)
            row = pl.multiple_of((n * NZ + g * 8 + zi) * NY, NY)
            shear[pl.ds(row, NY), :] = ydiff(vx)[HALO : HALO + NY] + turned_diff(
                vy[HALO : HALO + NY], svy_in, lane_in - 16 * g
            )
            if not last:
                join = jnp.where(group == g, vx, join)
        if not last:
            spread = back_diff(svx, join, lane16) + ydiff(svy)
            updated(S, zs, spread + (S[VZ, zs + 1] - S[VZ, zs - 1]), rows)

    def looped(body):
        def one(zi, _):
            body(zi)
            return 0

        lax.fori_loop(0, 8, one, 0)

    def step(n, last):
        looped(velocities)
        wrap_planes(VZ)
        looped(lambda zi: pressures(n, last, zi))
        if not last:
            wrap_planes(PR)
        return 0

    lax.fori_loop(0, STEPS - 1, lambda n, _: step(n, False), 0)
    step(STEPS - 1, True)
    targets = [vel_o.at[0], vel_o.at[1], vel_o.at[2], pr_o, me_o]

    def put(zi):
        return [
            pltpu.make_async_copy(X.at[f, :, zi], dst.at[:, zi], sems.at[f, zi])
            for f, dst in enumerate(targets)
        ]

    def unload(zi, _):
        for f in range(len(targets)):
            for g in range(8):
                plane = E[f, g * 10 + zi + 1, HALO : HALO + NY]
                X[f, g, zi] = roll(plane, -(7 if f == VX else 8) - 16 * g)
        for c in put(zi):
            c.start()
        return 0

    lax.fori_loop(0, 8, unload, 0)

    def pick(i, _):
        for k in range(8):
            at = i * 8 + k
            c = cell[at]
            for n in range(STEPS):
                G[n, pl.ds(at, 1), :] = shear[pl.ds(n * NZ * NY + (c >> 7), 1), :]
            L[pl.ds(at, 1), :] = jnp.full((1, 128), (c + 7 + 16 * (c >> 15)) & 127, jnp.int32)
        return 0

    lax.fori_loop(0, 32, pick, 0)
    wanted = lanes((256, 128)) == L[...]
    listed = hot[...].astype(jnp.float32)
    spec = spectra[...]
    sums = []
    for n in range(STEPS):
        sample = jnp.sum(jnp.where(wanted, G[n], 0.0), axis=1, keepdims=True)
        spec = spec + sample * phase[n : n + 1, :]
        scaled = listed * sample
        high = scaled.astype(jnp.bfloat16).astype(jnp.float32)
        both = high + roll(scaled - high, 64)
        total = transposed_dot(both.astype(jnp.bfloat16), patch_weights[...])
        sums.append(total[:64] + total[64:])
    spec_o[...] = spec
    quarter = lanes((64, 128)) >> 5
    for j in range(16):
        block = slice(128 * (j // 4), 128 * (j // 4) + 128)
        packed = jnp.zeros((64, 128), jnp.float32)
        for n in range(STEPS):
            packed = jnp.where(quarter == n, roll(sums[n][:, block], 32 * (n - j % 4)), packed)
        sums_o[:, j] = packed.reshape(8, 8, 128)
    for zi in range(8):
        for c in put(zi):
            c.wait()


def phase_rows(freqs):
    angle = np.pi * (np.arange(freqs) + 0.5) / freqs * np.arange(1, STEPS + 1)[:, None]
    return np.concatenate([np.cos(angle), -np.sin(angle)], axis=1).astype(np.float32)


def four_steps(velocity, fields, spectra, patch_cell, hot, patch_weights, halos):
    any_spec = pl.BlockSpec(memory_space=pl.ANY)
    vmem = pl.BlockSpec(memory_space=pltpu.VMEM)
    smem = pl.BlockSpec(memory_space=pltpu.SMEM)
    field = jax.ShapeDtypeStruct((8, 8, NY, NX), jnp.float32)
    vel, pr, me, spec, sums = pl.pallas_call(
        steps_kernel,
        out_shape=(
            jax.ShapeDtypeStruct((3, 8, 8, NY, NX), jnp.float32),
            field,
            field,
            jax.ShapeDtypeStruct(spectra.shape, jnp.float32),
            jax.ShapeDtypeStruct((8, 16, 8, 128), jnp.float32),
        ),
        in_specs=[smem] + [any_spec] * 7 + [vmem] * 9,
        out_specs=(any_spec, any_spec, any_spec, vmem, vmem),
        scratch_shapes=[
            pltpu.VMEM((FIELDS + 1, 80, EY, 128), jnp.float32),
            pltpu.VMEM((FIELDS + 1, 10, EY, 128), jnp.float32),
            pltpu.VMEM((FIELDS, 8, 8, NY, 128), jnp.float32),
            pltpu.VMEM((2, FIELDS, 64, 128), jnp.float32),
            pltpu.VMEM((STEPS * NZ * NY, 128), jnp.float32),
            pltpu.VMEM((STEPS, 256, 128), jnp.float32),
            pltpu.VMEM((256, 128), jnp.int32),
            pltpu.SemaphoreType.DMA((FIELDS, 8)),
        ],
        compiler_params=pltpu.CompilerParams(vmem_limit_bytes=56 * 1024 * 1024),
        name="four_steps",
    )(
        patch_cell,
        velocity.reshape(3, 8, 8, NY, NX),
        *[f.reshape(8, 8, NY, NX) for f in fields],
        spectra,
        jnp.asarray(phase_rows(spectra.shape[1] // 2)),
        hot,
        patch_weights,
        *halos,
    )
    shape = (NZ, NY, NX)
    return vel.reshape(velocity.shape), pr.reshape(shape), me.reshape(shape), spec, sums


def join_kernel(left, right, side, low, high):
    from_left = (lanes((NY, 128)) & 15) < 8

    def one(zi, _):
        lows, highs = [], []
        for f in range(FIELDS):
            strip = jnp.where(
                from_left, left[zi, f].astype(jnp.float32), right[zi, f].astype(jnp.float32)
            )
            side[zi, f] = strip.astype(jnp.bfloat16)
            lows.append(strip[:HALO])
            highs.append(strip[NY - HALO :])
        low[zi] = jnp.concatenate(lows, axis=0).astype(jnp.bfloat16)
        high[zi] = jnp.concatenate(highs, axis=0).astype(jnp.bfloat16)
        return 0

    lax.fori_loop(0, 8, one, 0)


def halo_exchange(velocity, fields):
    lo, hi, q = pack(velocity, *fields)
    yprev = shifted(hi, "gy", True)
    ynext = shifted(lo, "gy", False)
    left = shifted(q, "gx", True)
    right = shifted(q, "gx", False)
    side, low, high = small_call(
        join_kernel,
        [(q.shape, jnp.bfloat16)] + [((8, FIELDS * HALO, 128), jnp.bfloat16)] * 2,
        "join",
        (),
        0,
        2,
    )(left, right)
    cprev = shifted(high, "gy", True)
    cnext = shifted(low, "gy", False)
    return yprev, ynext, side, cprev, cnext


def rows_of(shape):
    return lax.broadcasted_iota(jnp.int32, shape, 0)


def transposed_dot(a, b):
    return lax.dot_general(a, b, (((0,), (0,)), ((), ())), preferred_element_type=jnp.float32)


def as_row(column, n):
    eye = rows_of((n, n)) == lanes((n, n))
    return jnp.sum(jnp.where(eye, column, 0.0), axis=0, keepdims=True)


def as_column(row, n):
    eye = rows_of((n, n)) == lanes((n, n))
    return jnp.sum(jnp.where(eye, row, 0.0), axis=1, keepdims=True)


def route_kernel(table, spectra, weights, send, place, pick, hot, turned, stage):
    n = spectra.shape[0]
    gx, gy = lax.axis_index("gx"), lax.axis_index("gy")
    base = (gx * 16 + gy) * n
    mine = table[pl.ds(pl.multiple_of(gx * 8, 8), 8), :].astype(jnp.float32)
    mine = pltpu.roll(mine, lax.rem(512 - 32 * gy, 512), 1)[:, :128]
    quarter = lanes((1, 128)) >> 5
    halves = []
    for h in range(2):
        half = jnp.zeros((1, 128), jnp.float32)
        for q in range(4):
            r = 4 * h + q
            half = jnp.where(quarter == q, roll(mine, 32 * q)[r : r + 1], half)
        halves.append(half)
    ids_r = jnp.concatenate(halves, axis=1)
    ids = as_column(ids_r, n).astype(jnp.int32)
    ids_r = ids_r.astype(jnp.int32)
    columns = []
    for chunk in range(n // 32):
        own = base + chunk * 32 + rows_of((32, 512))

        def search(r8, found):
            for k in range(8):
                r = r8 * 8 + k
                found = jnp.where(table[pl.ds(r, 1), :] == own, r, found)
            return found

        found = lax.fori_loop(0, table.shape[0] // 8, search, jnp.full((32, 512), -1, jnp.int32))
        slot = jnp.where(found >= 0, found * 512 + lanes((32, 512)), -1).astype(jnp.float32)
        columns.append(jnp.max(slot, axis=1, keepdims=True))
    slot = jnp.concatenate(columns, axis=0).astype(jnp.int32)
    rupture = slot >> 9
    target = (((rupture >> 3) << 4) + ((slot & 511) >> 5)).astype(jnp.float32)
    hot[...] = (lanes((n, 128)) == rupture).astype(jnp.float32).astype(jnp.bfloat16)
    target_row = as_row(target, n)
    before = rows_of((n, n)) < lanes((n, n))
    rank = jnp.sum(
        jnp.where((target == target_row) & before, 1.0, 0.0), axis=0, keepdims=True
    )
    same = (ids >> 8) == (ids_r >> 8)
    rank_in = jnp.sum(jnp.where(same & (ids < ids_r), 1.0, 0.0), axis=0, keepdims=True)
    device = rows_of((128, n))
    target_row = target_row.astype(jnp.int32)
    source_row = ids_r >> 8
    stage[...] = jnp.zeros_like(stage)
    rounded = spectra[...].astype(jnp.bfloat16)
    for k in range(CAP):
        to = jnp.where((device == target_row) & (rank == k), 1.0, 0.0).astype(jnp.bfloat16)
        back = jnp.where((device == source_row) & (rank_in == k), 1.0, 0.0).astype(jnp.bfloat16)
        place[k] = to
        pick[k] = back
        sent = jnp.dot(to, rounded, preferred_element_type=jnp.float32)
        sent_w = jnp.dot(back, weights[...], preferred_element_type=jnp.float32)
        for c in range(2):
            stage[pl.ds(6 * k + c, 128, stride=16), :] = sent[:, 128 * c : 128 * (c + 1)]
        for c in range(4):
            stage[pl.ds(6 * k + 2 + c, 128, stride=16), :] = sent_w[:, 128 * c : 128 * (c + 1)]
    send[...] = stage[...].astype(jnp.bfloat16).reshape(send.shape)
    eye = (rows_of((n, n)) == lanes((n, n))).astype(jnp.float32).astype(jnp.bfloat16)
    turned[...] = transposed_dot(weights[...], eye).astype(jnp.bfloat16).reshape(turned.shape)


def sort_kernel(received, place, pick, turned, message, patch_weights, stage):
    stage[...] = received[...].reshape(stage.shape).astype(jnp.float32)
    spectra = jnp.zeros((256, 256), jnp.float32)
    mine = jnp.zeros((256, 512), jnp.float32)
    for k in range(CAP):
        parts = [
            stage[pl.ds(6 * k + c, 128, stride=16), :].astype(jnp.bfloat16) for c in range(6)
        ]
        spectra += transposed_dot(pick[k], jnp.concatenate(parts[:2], axis=1))
        mine += transposed_dot(place[k], jnp.concatenate(parts[2:], axis=1))
    patch_weights[...] = mine.astype(jnp.bfloat16)
    for j in range(16):
        message[j, :256] = spectra.astype(jnp.bfloat16)
        message[j, 256:] = turned[j]


def product_kernel(gathered, out):
    square = (256, 256)
    same = ((rows_of(square) >> 5) == (lanes(square) >> 5)).astype(jnp.float32)
    same = same.astype(jnp.bfloat16)
    total = jnp.zeros(square, jnp.float32)
    for j in range(16):
        spread = jnp.concatenate([gathered[j, 256:]] * 8, axis=0) * same
        total += jnp.dot(spread, gathered[j, :256], preferred_element_type=jnp.float32)
    out[...] = total


def slip_kernel(product, sums, phase, out):
    total = jnp.sum(sums[...], axis=0)
    own = (lanes((32, 128)) & 31) == rows_of((32, 128))
    left = jnp.concatenate(
        [jnp.where(own, total[r : r + 1], 0.0) for r in range(8)], axis=0
    )
    added = jnp.dot(
        left, phase[...], precision=lax.Precision.HIGHEST, preferred_element_type=jnp.float32
    )
    out[...] = (product[...] + added).reshape(out.shape)


def small_call(kernel, outs, name, scratch=(), smem=0, inputs=0):
    vmem = pl.BlockSpec(memory_space=pltpu.VMEM)
    specs = [pl.BlockSpec(memory_space=pltpu.SMEM)] * smem + [vmem] * (inputs - smem)
    shapes = tuple(jax.ShapeDtypeStruct(s, d) for s, d in outs)
    return pl.pallas_call(
        kernel,
        out_shape=shapes,
        in_specs=specs,
        out_specs=(vmem,) * len(shapes),
        scratch_shapes=scratch,
        name=name,
    )


def routed(spectra, rupture_patches, slip_weights):
    bf16, f32 = jnp.bfloat16, jnp.float32
    tiles = (128, 16, 128)
    return small_call(
        route_kernel,
        [
            (tiles, bf16),
            ((2, 128, 256), bf16),
            ((2, 128, 256), bf16),
            ((256, 128), bf16),
            ((16, 32, 256), bf16),
        ],
        "route",
        [pltpu.VMEM((2048, 128), f32)],
        0,
        3,
    )(rupture_patches, spectra, slip_weights.reshape(256, 512))


def sorted_rows(received, place, pick, turned):
    return small_call(
        sort_kernel,
        [((16, 288, 256), jnp.bfloat16), ((256, 512), jnp.bfloat16)],
        "sort",
        [pltpu.VMEM((2048, 128), jnp.float32)],
        0,
        4,
    )(received, place, pick, turned)


def slip_response(gathered, sums):
    f32 = jnp.float32
    sums, gathered = lax.optimization_barrier((sums, gathered))
    sums = lax.all_to_all(sums.reshape(128, 8, 128), ("gx", "gy"), 0, 0, tiled=True)
    (product,) = small_call(product_kernel, [((256, 256), f32)], "product", (), 0, 1)(gathered)
    phase = jnp.asarray(np.repeat(phase_rows(128), 32, axis=0))
    (slip,) = small_call(slip_kernel, [((8, 32, 256), f32)], "slip", (), 0, 3)(
        product, sums, phase
    )
    return slip


def per_device(
    velocity,
    pressure,
    memory,
    buoyancy,
    modulus,
    relax,
    strength,
    spectra,
    patch_cell,
    rupture_patches,
    slip_weights,
):
    fields = (pressure, memory, buoyancy, modulus, relax, strength)
    halos = halo_exchange(velocity, fields)
    send, place, pick, hot, turned = routed(spectra, rupture_patches, slip_weights)
    received = lax.all_to_all(send, ("gx", "gy"), 0, 0, tiled=True)
    received, _ = lax.optimization_barrier((received, halos))
    message, patch_weights = sorted_rows(received, place, pick, turned)
    gathered = lax.all_to_all(message, "gy", 0, 0, tiled=True)
    spectra, message = lax.optimization_barrier((spectra, message))
    velocity, pressure, memory, spectra, sums = four_steps(
        velocity, fields, spectra, patch_cell, hot, patch_weights, halos
    )
    slip = slip_response(gathered, sums)
    return (velocity, pressure, memory, spectra, slip)


def solution(mesh):
    field = P(None, "gy", "gx")
    in_specs = (
        (P(None, None, "gy", "gx"),)
        + (field,) * 6
        + (P(("gx", "gy"), None), P(("gx", "gy")), P(), P("gx", "gy", None))
    )
    out_specs = (
        P(None, None, "gy", "gx"),
        field,
        field,
        P(("gx", "gy"), None),
        P("gx", "gy", None),
    )
    return jax.shard_map(
        per_device, mesh=mesh, in_specs=in_specs, out_specs=out_specs, check_vma=False
    )
```

```python
import jax
import jax.numpy as jnp
import numpy as np
from jax import lax
from jax.experimental import pallas as pl
from jax.experimental.pallas import tpu as pltpu
from jax.sharding import PartitionSpec as P

STEPS = 4
CAP = 2
NZ, NY, NX = 64, 32, 128
HALO = 8
EY = NY + 2 * HALO
FIELDS = 9
VX, VY, VZ, PR, ME, BU, MO, RE, ST = range(FIELDS)
BP = FIELDS
AHEAD = 6
REACH = [7, 7, 6, 8, 6, 7, 6, 6, 6]
SENT = [(f, d) for f in range(FIELDS) for d in range(REACH[f])]
ROWS = 8 * (len(SENT) + len(SENT) % 2)


def lanes(shape):
    return lax.broadcasted_iota(jnp.int32, shape, len(shape) - 1)


def roll(x, shift, axis=1):
    shift = shift % x.shape[axis]
    return pltpu.roll(x, shift, axis) if shift else x


def pack_kernel(
    vel, pr, me, bu, mo, re, st, turn, lo_o, hi_o, q_o, X, lo_s, hi_s, q_s, lows, highs, sems, done
):
    sources = [vel.at[0], vel.at[1], vel.at[2], pr, me, bu, mo, re, st]

    def fetch(zi):
        return [
            pltpu.make_async_copy(src.at[:, zi], X.at[f, :, zi], sems.at[f, zi])
            for f, src in enumerate(sources)
        ]

    def put(zi):
        return [
            pltpu.make_async_copy(src.at[zi], dst.at[zi], done.at[k, zi])
            for k, (src, dst) in enumerate(((lo_s, lo_o), (hi_s, hi_o), (q_s, q_o)))
        ]

    for zi in range(AHEAD):
        for c in fetch(zi):
            c.start()
    lane = lanes((NY, 128))

    def one(zi, _):
        @pl.when(zi + AHEAD < 8)
        def _():
            for c in fetch(zi + AHEAD):
                c.start()

        copies = fetch(zi)
        for c in copies:
            c.wait()
        strips = jnp.zeros((FIELDS * NY, 128), jnp.float32)
        for g in range(8):
            planes = [X[f, g, zi] for f in range(FIELDS)]
            for f, plane in enumerate(planes):
                shift = (7 if f == VX else 8) + 16 * g
                lows[f, pl.ds(8 * g, 8)] = roll(plane[:HALO], shift)
                highs[f, pl.ds(8 * g, 8)] = roll(plane[NY - HALO :], shift)
            planes = jnp.concatenate(planes, axis=0).astype(jnp.bfloat16)
            strips += jnp.dot(planes, turn[g], preferred_element_type=jnp.float32)
        q_s[zi] = strips.astype(jnp.bfloat16).reshape(FIELDS, NY, 128)
        for ref, ends, first in ((lo_s, lows, False), (hi_s, highs, True)):
            tiles = [
                ends[f, pl.ds(d + (HALO - REACH[f] if first else 0), 8, stride=8)]
                for f, d in SENT
            ]
            if len(tiles) % 2:
                tiles.append(tiles[-1])
            for t in range(0, len(tiles), 2):
                pair = jnp.concatenate(tiles[t : t + 2], axis=0)
                ref[zi, pl.ds(8 * t, 16)] = pair.astype(jnp.bfloat16)
        for c in put(zi):
            c.start()
        return 0

    lax.fori_loop(0, 8, one, 0)
    for zi in range(8):
        for c in put(zi):
            c.wait()


def pack(velocity, *fields):
    lane = np.arange(128)
    turn = np.zeros((8, 128, 128), np.float32)
    for g in range(8):
        own = lane[lane >> 4 == g]
        turn[g, (own - 8 - 16 * g) % 128, own] = 1
    any_spec = pl.BlockSpec(memory_space=pl.ANY)
    yshape, qshape = (8, ROWS, 128), (8, FIELDS, NY, 128)
    return pl.pallas_call(
        pack_kernel,
        out_shape=tuple(jax.ShapeDtypeStruct(s, jnp.bfloat16) for s in (yshape, yshape, qshape)),
        in_specs=[any_spec] * 7 + [pl.BlockSpec(memory_space=pltpu.VMEM)],
        out_specs=(any_spec,) * 3,
        scratch_shapes=[
            pltpu.VMEM((FIELDS, 8, 8, NY, 128), jnp.float32),
            pltpu.VMEM(yshape, jnp.bfloat16),
            pltpu.VMEM(yshape, jnp.bfloat16),
            pltpu.VMEM(qshape, jnp.bfloat16),
            pltpu.VMEM((FIELDS, 64, 128), jnp.float32),
            pltpu.VMEM((FIELDS, 64, 128), jnp.float32),
            pltpu.SemaphoreType.DMA((FIELDS, 8)),
            pltpu.SemaphoreType.DMA((3, 8)),
        ],
        compiler_params=pltpu.CompilerParams(vmem_limit_bytes=56 * 1024 * 1024),
        name="pack",
    )(
        velocity.reshape(3, 8, 8, NY, NX),
        *[f.reshape(8, 8, NY, NX) for f in fields],
        jnp.asarray(turn, jnp.bfloat16),
    )


def shifted(array, axis, up):
    n = lax.axis_size(axis)
    pairs = [(i, i + 1) if up else (i + 1, i) for i in range(n - 1)]
    return lax.ppermute(array, axis, pairs)


def ydiff(x):
    return roll(x, -1, 0) - roll(x, 1, 0)


def turned_diff(x, other, at):
    return roll(jnp.where(at == 8, other, x), -2) - jnp.where(at == 7, other, x)


def back_diff(x, other, at):
    return jnp.where(at == 7, other, x) - roll(jnp.where(at == 6, other, x), 2)


def steps_kernel(
    cell,
    vel,
    pr,
    me,
    bu,
    mo,
    re,
    st,
    spectra,
    phase,
    hot,
    patch_weights,
    yprev,
    ynext,
    left,
    right,
    cprev,
    cnext,
    vel_o,
    pr_o,
    me_o,
    spec_o,
    sums_o,
    E,
    S,
    X,
    T,
    shear,
    G,
    L,
    sems,
):
    sources = [vel.at[0], vel.at[1], vel.at[2], pr, me, bu, mo, re, st]

    def fetch(zi):
        return [
            pltpu.make_async_copy(src.at[:, zi], X.at[f, :, zi], sems.at[f, zi])
            for f, src in enumerate(sources)
        ]

    for zi in range(AHEAD):
        for c in fetch(zi):
            c.start()
    lane = lanes((EY, 128))
    lane16 = lane & 15
    group = lane >> 4
    zero = jnp.zeros((EY, 128), jnp.float32)

    def fill(zi):
        cp = cprev[zi].astype(jnp.float32)
        cn = cnext[zi].astype(jnp.float32)
        for ref, ends, first in ((ynext, T.at[0], False), (yprev, T.at[1], True)):
            for t in range(0, len(SENT), 2):
                pair = ref[zi, pl.ds(8 * t, 16)].astype(jnp.float32)
                for k, (f, d) in enumerate(SENT[t : t + 2]):
                    at = d + (HALO - REACH[f] if first else 0)
                    ends[f, pl.ds(at, 8, stride=8)] = pair[8 * k : 8 * k + 8]
        for f in range(FIELDS):
            for g in range(8):
                z = g * 10 + zi + 1
                low, high = T[1, f, pl.ds(8 * g, 8)], T[0, f, pl.ds(8 * g, 8)]
                mid = roll(X[f, g, zi], (7 if f == VX else 8) + 16 * g)
                E[f, z, :HALO] = low
                E[f, z, HALO + NY :] = high
                E[f, z, HALO : HALO + NY] = mid
                if f == BU:
                    E[BP, z, :HALO] = roll(low, -1)
                    E[BP, z, HALO + NY :] = roll(high, -1)
                    E[BP, z, HALO : HALO + NY] = roll(mid, -1)
            low, high = cp[8 * f : 8 * f + 8], cn[8 * f : 8 * f + 8]
            mid = jnp.where(
                lane16[:NY] < 8, left[zi, f].astype(jnp.float32), right[zi, f].astype(jnp.float32)
            )
            if f in (VX, BU):
                to = VX if f == VX else BP
                S[to, zi + 1, :HALO] = roll(low, -1)
                S[to, zi + 1, HALO + NY :] = roll(high, -1)
                S[to, zi + 1, HALO : HALO + NY] = roll(mid, -1)
            if f != VX:
                S[f, zi + 1, :HALO] = low
                S[f, zi + 1, HALO + NY :] = high
                S[f, zi + 1, HALO : HALO + NY] = mid

    def wrap_planes(f):
        S[f, 0] = jnp.where(lane < 16, 0.0, roll(S[f, 8], 16))
        S[f, 9] = jnp.where(lane >= 112, 0.0, roll(S[f, 1], -16))
        for g in range(8):
            E[f, 10 * g] = roll(E[f, 10 * g - 2], 16) if g else zero
            E[f, 10 * g + 9] = roll(E[f, 10 * g + 11], -16) if g < 7 else zero

    T[...] = jnp.zeros_like(T)
    def load(zi, _):
        @pl.when(zi + AHEAD < 8)
        def _():
            for c in fetch(zi + AHEAD):
                c.start()

        for c in fetch(zi):
            c.wait()
        fill(zi)
        return 0

    lax.fori_loop(0, 8, load, 0)
    wrap_planes(PR)

    def moved(ref, z, dx, p):
        ref[VX, z] = ref[VX, z] - ref[BP, z] * dx
        b = ref[BU, z]
        ref[VY, z] = ref[VY, z] - b * ydiff(p)
        ref[VZ, z] = ref[VZ, z] - b * (ref[PR, z + 1] - ref[PR, z - 1])

    def velocities(zi):
        zs = zi + 1
        ps = S[PR, zs]
        join = zero
        for g in range(8):
            z = g * 10 + zi + 1
            p = E[PR, z]
            moved(E, z, turned_diff(p, ps, lane - 16 * g), p)
            join = jnp.where(group == g, p, join)
        moved(S, zs, turned_diff(ps, join, lane16), ps)

    def updated(ref, z, spread, rows):
        m = ref[ME, z, rows]
        m = m - ref[RE, z, rows] * (m + ref[ST, z, rows] * spread)
        ref[ME, z, rows] = m
        ref[PR, z, rows] = ref[PR, z, rows] - ref[MO, z, rows] * (spread + m)

    def pressures(n, last, zi):
        zs = zi + 1
        rows = slice(HALO, HALO + NY) if last else slice(0, EY)
        svx, svy = S[VX, zs], S[VY, zs]
        svy_in = svy[HALO : HALO + NY]
        lane_in = lane[:NY]
        join = zero
        for g in range(8):
            z = g * 10 + zi + 1
            vx, vy = E[VX, z], E[VY, z]
            spread = back_diff(vx[rows], svx[rows], lane[rows] - 16 * g) + ydiff(vy)[rows]
            updated(E, z, spread + (E[VZ, z + 1, rows] - E[VZ, z - 1, rows]), rows)
            row = pl.multiple_of((n * NZ + g * 8 + zi) * NY, NY)
            shear[pl.ds(row, NY), :] = ydiff(vx)[HALO : HALO + NY] + turned_diff(
                vy[HALO : HALO + NY], svy_in, lane_in - 16 * g
            )
            if not last:
                join = jnp.where(group == g, vx, join)
        if not last:
            spread = back_diff(svx, join, lane16) + ydiff(svy)
            updated(S, zs, spread + (S[VZ, zs + 1] - S[VZ, zs - 1]), rows)

    def looped(body):
        def one(zi, _):
            body(zi)
            return 0

        lax.fori_loop(0, 8, one, 0)

    def step(n, last):
        looped(velocities)
        wrap_planes(VZ)
        looped(lambda zi: pressures(n, last, zi))
        if not last:
            wrap_planes(PR)
        return 0

    lax.fori_loop(0, STEPS - 1, lambda n, _: step(n, False), 0)
    step(STEPS - 1, True)
    targets = [vel_o.at[0], vel_o.at[1], vel_o.at[2], pr_o, me_o]

    def put(zi):
        return [
            pltpu.make_async_copy(X.at[f, :, zi], dst.at[:, zi], sems.at[f, zi])
            for f, dst in enumerate(targets)
        ]

    def unload(zi, _):
        for f in range(len(targets)):
            for g in range(8):
                plane = E[f, g * 10 + zi + 1, HALO : HALO + NY]
                X[f, g, zi] = roll(plane, -(7 if f == VX else 8) - 16 * g)
        for c in put(zi):
            c.start()
        return 0

    lax.fori_loop(0, 8, unload, 0)

    def pick(i, _):
        for k in range(8):
            at = i * 8 + k
            c = cell[at]
            for n in range(STEPS):
                G[n, pl.ds(at, 1), :] = shear[pl.ds(n * NZ * NY + (c >> 7), 1), :]
            L[pl.ds(at, 1), :] = jnp.full((1, 128), (c + 7 + 16 * (c >> 15)) & 127, jnp.int32)
        return 0

    lax.fori_loop(0, 32, pick, 0)
    wanted = lanes((256, 128)) == L[...]
    listed = hot[...].astype(jnp.float32)
    spec = spectra[...]
    sums = []
    for n in range(STEPS):
        sample = jnp.sum(jnp.where(wanted, G[n], 0.0), axis=1, keepdims=True)
        spec = spec + sample * phase[n : n + 1, :]
        scaled = listed * sample
        high = scaled.astype(jnp.bfloat16).astype(jnp.float32)
        both = high + roll(scaled - high, 64)
        total = transposed_dot(both.astype(jnp.bfloat16), patch_weights[...])
        sums.append(total[:64] + total[64:])
    spec_o[...] = spec
    quarter = lanes((64, 128)) >> 5
    for j in range(16):
        block = slice(128 * (j // 4), 128 * (j // 4) + 128)
        packed = jnp.zeros((64, 128), jnp.float32)
        for n in range(STEPS):
            packed = jnp.where(quarter == n, roll(sums[n][:, block], 32 * (n - j % 4)), packed)
        sums_o[:, j] = packed.reshape(8, 8, 128)
    for zi in range(8):
        for c in put(zi):
            c.wait()


def phase_rows(freqs):
    angle = np.pi * (np.arange(freqs) + 0.5) / freqs * np.arange(1, STEPS + 1)[:, None]
    return np.concatenate([np.cos(angle), -np.sin(angle)], axis=1).astype(np.float32)


def four_steps(velocity, fields, spectra, patch_cell, hot, patch_weights, halos):
    any_spec = pl.BlockSpec(memory_space=pl.ANY)
    vmem = pl.BlockSpec(memory_space=pltpu.VMEM)
    smem = pl.BlockSpec(memory_space=pltpu.SMEM)
    field = jax.ShapeDtypeStruct((8, 8, NY, NX), jnp.float32)
    vel, pr, me, spec, sums = pl.pallas_call(
        steps_kernel,
        out_shape=(
            jax.ShapeDtypeStruct((3, 8, 8, NY, NX), jnp.float32),
            field,
            field,
            jax.ShapeDtypeStruct(spectra.shape, jnp.float32),
            jax.ShapeDtypeStruct((8, 16, 8, 128), jnp.float32),
        ),
        in_specs=[smem] + [any_spec] * 7 + [vmem] * 10,
        out_specs=(any_spec, any_spec, any_spec, vmem, vmem),
        scratch_shapes=[
            pltpu.VMEM((FIELDS + 1, 80, EY, 128), jnp.float32),
            pltpu.VMEM((FIELDS + 1, 10, EY, 128), jnp.float32),
            pltpu.VMEM((FIELDS, 8, 8, NY, 128), jnp.float32),
            pltpu.VMEM((2, FIELDS, 64, 128), jnp.float32),
            pltpu.VMEM((STEPS * NZ * NY, 128), jnp.float32),
            pltpu.VMEM((STEPS, 256, 128), jnp.float32),
            pltpu.VMEM((256, 128), jnp.int32),
            pltpu.SemaphoreType.DMA((FIELDS, 8)),
        ],
        compiler_params=pltpu.CompilerParams(vmem_limit_bytes=56 * 1024 * 1024),
        name="four_steps",
    )(
        patch_cell,
        velocity.reshape(3, 8, 8, NY, NX),
        *[f.reshape(8, 8, NY, NX) for f in fields],
        spectra,
        jnp.asarray(phase_rows(spectra.shape[1] // 2)),
        hot,
        patch_weights,
        *halos,
    )
    shape = (NZ, NY, NX)
    return vel.reshape(velocity.shape), pr.reshape(shape), me.reshape(shape), spec, sums


def join_kernel(left, right, low, high):
    from_left = (lanes((NY, 128)) & 15) < 8

    def one(zi, _):
        lows, highs = [], []
        for f in range(FIELDS):
            strip = jnp.where(
                from_left, left[zi, f].astype(jnp.float32), right[zi, f].astype(jnp.float32)
            )
            lows.append(strip[:HALO])
            highs.append(strip[NY - HALO :])
        low[zi] = jnp.concatenate(lows, axis=0).astype(jnp.bfloat16)
        high[zi] = jnp.concatenate(highs, axis=0).astype(jnp.bfloat16)
        return 0

    lax.fori_loop(0, 8, one, 0)


def halo_exchange(velocity, fields):
    lo, hi, q = pack(velocity, *fields)
    yprev = shifted(hi, "gy", True)
    ynext = shifted(lo, "gy", False)
    left = shifted(q, "gx", True)
    right = shifted(q, "gx", False)
    low, high = small_call(
        join_kernel,
        [((8, FIELDS * HALO, 128), jnp.bfloat16)] * 2,
        "join",
        (),
        0,
        2,
    )(left, right)
    cprev = shifted(high, "gy", True)
    cnext = shifted(low, "gy", False)
    return yprev, ynext, left, right, cprev, cnext


def rows_of(shape):
    return lax.broadcasted_iota(jnp.int32, shape, 0)


def transposed_dot(a, b):
    return lax.dot_general(a, b, (((0,), (0,)), ((), ())), preferred_element_type=jnp.float32)


def as_row(column, n):
    eye = rows_of((n, n)) == lanes((n, n))
    return jnp.sum(jnp.where(eye, column, 0.0), axis=0, keepdims=True)


def as_column(row, n):
    eye = rows_of((n, n)) == lanes((n, n))
    return jnp.sum(jnp.where(eye, row, 0.0), axis=1, keepdims=True)


def route_kernel(table, spectra, weights, send, place, pick, hot, turned, stage):
    n = spectra.shape[0]
    gx, gy = lax.axis_index("gx"), lax.axis_index("gy")
    base = (gx * 16 + gy) * n
    mine = table[pl.ds(pl.multiple_of(gx * 8, 8), 8), :].astype(jnp.float32)
    mine = pltpu.roll(mine, lax.rem(512 - 32 * gy, 512), 1)[:, :128]
    quarter = lanes((1, 128)) >> 5
    halves = []
    for h in range(2):
        half = jnp.zeros((1, 128), jnp.float32)
        for q in range(4):
            r = 4 * h + q
            half = jnp.where(quarter == q, roll(mine, 32 * q)[r : r + 1], half)
        halves.append(half)
    ids_r = jnp.concatenate(halves, axis=1)
    ids = as_column(ids_r, n).astype(jnp.int32)
    ids_r = ids_r.astype(jnp.int32)
    columns = []
    for chunk in range(n // 32):
        own = base + chunk * 32 + rows_of((32, 512))

        def search(r8, found):
            for k in range(8):
                r = r8 * 8 + k
                found = jnp.where(table[pl.ds(r, 1), :] == own, r, found)
            return found

        found = lax.fori_loop(0, table.shape[0] // 8, search, jnp.full((32, 512), -1, jnp.int32))
        slot = jnp.where(found >= 0, found * 512 + lanes((32, 512)), -1).astype(jnp.float32)
        columns.append(jnp.max(slot, axis=1, keepdims=True))
    slot = jnp.concatenate(columns, axis=0).astype(jnp.int32)
    rupture = slot >> 9
    target = (((rupture >> 3) << 4) + ((slot & 511) >> 5)).astype(jnp.float32)
    hot[...] = (lanes((n, 128)) == rupture).astype(jnp.float32).astype(jnp.bfloat16)
    target_row = as_row(target, n)
    before = rows_of((n, n)) < lanes((n, n))
    rank = jnp.sum(
        jnp.where((target == target_row) & before, 1.0, 0.0), axis=0, keepdims=True
    )
    same = (ids >> 8) == (ids_r >> 8)
    rank_in = jnp.sum(jnp.where(same & (ids < ids_r), 1.0, 0.0), axis=0, keepdims=True)
    device = rows_of((128, n))
    target_row = target_row.astype(jnp.int32)
    source_row = ids_r >> 8
    stage[...] = jnp.zeros_like(stage)
    rounded = spectra[...].astype(jnp.bfloat16)
    for k in range(CAP):
        to = jnp.where((device == target_row) & (rank == k), 1.0, 0.0).astype(jnp.bfloat16)
        back = jnp.where((device == source_row) & (rank_in == k), 1.0, 0.0).astype(jnp.bfloat16)
        place[k] = to
        pick[k] = back
        sent = jnp.dot(to, rounded, preferred_element_type=jnp.float32)
        sent_w = jnp.dot(back, weights[...], preferred_element_type=jnp.float32)
        for c in range(2):
            stage[pl.ds(6 * k + c, 128, stride=16), :] = sent[:, 128 * c : 128 * (c + 1)]
        for c in range(4):
            stage[pl.ds(6 * k + 2 + c, 128, stride=16), :] = sent_w[:, 128 * c : 128 * (c + 1)]
    send[...] = stage[...].astype(jnp.bfloat16).reshape(send.shape)
    eye = (rows_of((n, n)) == lanes((n, n))).astype(jnp.float32).astype(jnp.bfloat16)
    turned[...] = transposed_dot(weights[...], eye).astype(jnp.bfloat16).reshape(turned.shape)


def sort_kernel(received, place, pick, turned, message, patch_weights, stage):
    stage[...] = received[...].reshape(stage.shape).astype(jnp.float32)
    spectra = jnp.zeros((256, 256), jnp.float32)
    mine = jnp.zeros((256, 512), jnp.float32)
    for k in range(CAP):
        parts = [
            stage[pl.ds(6 * k + c, 128, stride=16), :].astype(jnp.bfloat16) for c in range(6)
        ]
        spectra += transposed_dot(pick[k], jnp.concatenate(parts[:2], axis=1))
        mine += transposed_dot(place[k], jnp.concatenate(parts[2:], axis=1))
    patch_weights[...] = mine.astype(jnp.bfloat16)
    for j in range(16):
        message[j, :256] = spectra.astype(jnp.bfloat16)
        message[j, 256:] = turned[j]


def product_kernel(gathered, out):
    square = (256, 256)
    same = ((rows_of(square) >> 5) == (lanes(square) >> 5)).astype(jnp.float32)
    same = same.astype(jnp.bfloat16)
    total = jnp.zeros(square, jnp.float32)
    for j in range(16):
        spread = jnp.concatenate([gathered[j, 256:]] * 8, axis=0) * same
        total += jnp.dot(spread, gathered[j, :256], preferred_element_type=jnp.float32)
    out[...] = total


def slip_kernel(product, sums, phase, out):
    total = jnp.sum(sums[...], axis=0)
    own = (lanes((32, 128)) & 31) == rows_of((32, 128))
    left = jnp.concatenate(
        [jnp.where(own, total[r : r + 1], 0.0) for r in range(8)], axis=0
    )
    added = jnp.dot(
        left, phase[...], precision=lax.Precision.HIGHEST, preferred_element_type=jnp.float32
    )
    out[...] = (product[...] + added).reshape(out.shape)


def small_call(kernel, outs, name, scratch=(), smem=0, inputs=0):
    vmem = pl.BlockSpec(memory_space=pltpu.VMEM)
    specs = [pl.BlockSpec(memory_space=pltpu.SMEM)] * smem + [vmem] * (inputs - smem)
    shapes = tuple(jax.ShapeDtypeStruct(s, d) for s, d in outs)
    return pl.pallas_call(
        kernel,
        out_shape=shapes,
        in_specs=specs,
        out_specs=(vmem,) * len(shapes),
        scratch_shapes=scratch,
        name=name,
    )


def routed(spectra, rupture_patches, slip_weights):
    bf16, f32 = jnp.bfloat16, jnp.float32
    tiles = (128, 16, 128)
    return small_call(
        route_kernel,
        [
            (tiles, bf16),
            ((2, 128, 256), bf16),
            ((2, 128, 256), bf16),
            ((256, 128), bf16),
            ((16, 32, 256), bf16),
        ],
        "route",
        [pltpu.VMEM((2048, 128), f32)],
        0,
        3,
    )(rupture_patches, spectra, slip_weights.reshape(256, 512))


def sorted_rows(received, place, pick, turned):
    return small_call(
        sort_kernel,
        [((16, 288, 256), jnp.bfloat16), ((256, 512), jnp.bfloat16)],
        "sort",
        [pltpu.VMEM((2048, 128), jnp.float32)],
        0,
        4,
    )(received, place, pick, turned)


def slip_response(gathered, sums):
    f32 = jnp.float32
    sums, gathered = lax.optimization_barrier((sums, gathered))
    sums = lax.all_to_all(sums.reshape(128, 8, 128), ("gx", "gy"), 0, 0, tiled=True)
    (product,) = small_call(product_kernel, [((256, 256), f32)], "product", (), 0, 1)(gathered)
    phase = jnp.asarray(np.repeat(phase_rows(128), 32, axis=0))
    (slip,) = small_call(slip_kernel, [((8, 32, 256), f32)], "slip", (), 0, 3)(
        product, sums, phase
    )
    return slip


def per_device(
    velocity,
    pressure,
    memory,
    buoyancy,
    modulus,
    relax,
    strength,
    spectra,
    patch_cell,
    rupture_patches,
    slip_weights,
):
    fields = (pressure, memory, buoyancy, modulus, relax, strength)
    halos = halo_exchange(velocity, fields)
    send, place, pick, hot, turned = routed(spectra, rupture_patches, slip_weights)
    received = lax.all_to_all(send, ("gx", "gy"), 0, 0, tiled=True)
    received, _ = lax.optimization_barrier((received, halos))
    message, patch_weights = sorted_rows(received, place, pick, turned)
    gathered = lax.all_to_all(message, "gy", 0, 0, tiled=True)
    spectra, message = lax.optimization_barrier((spectra, message))
    velocity, pressure, memory, spectra, sums = four_steps(
        velocity, fields, spectra, patch_cell, hot, patch_weights, halos
    )
    slip = slip_response(gathered, sums)
    return (velocity, pressure, memory, spectra, slip)


def solution(mesh):
    field = P(None, "gy", "gx")
    in_specs = (
        (P(None, None, "gy", "gx"),)
        + (field,) * 6
        + (P(("gx", "gy"), None), P(("gx", "gy")), P(), P("gx", "gy", None))
    )
    out_specs = (
        P(None, None, "gy", "gx"),
        field,
        field,
        P(("gx", "gy"), None),
        P("gx", "gy", None),
    )
    return jax.shard_map(
        per_device, mesh=mesh, in_specs=in_specs, out_specs=out_specs, check_vma=False
    )
```
